32 devices in a mesh: hel: 4 (over y, core), rad: 8 (over z, x).
Axes of the slice: x: 2, y: 2, z: 4, core: 2. Of those that a mesh axis runs over, the one named last changes fastest.
Arguments:
- older_packet: float32 [4, 512, 8, 1024], P('hel', 'rad'), may hold values from -6 to 6
- newer_packet: float32 [4, 512, 8, 1024], P('hel', 'rad'), may hold values from -6 to 6
- kinetic: bfloat16 [512, 512], replicated, may hold values from -1 to 1, as said below
- transform: bfloat16 [4, 1024, 1024], P('hel'), may hold values from -0.1875 to 0.1875
- potential: bfloat16 [512, 8, 1024], P('rad'), may hold values from -2 to 2
- coupling: bfloat16 [4, 1024], P('hel'), may hold values from 0.29882812 to 1.5
- radial_weight: float32 [512], replicated, may hold values from 0.3 to 2
- damping: float32 [512], P('rad'), may hold values from 0.6 to 1
Outputs:
- older_out: float32 [4, 512, 8, 1024], P('hel', 'rad')
- newer_out: float32 [4, 512, 8, 1024], P('hel', 'rad')
The draws below stay inside these ranges and needn't reach their ends.
Inputs may be any that keep to these rules, and one draw needn't show every extreme that they name: kinetic is symmetric.
All inputs are finite; a program needn't handle non-finite values.
Results may differ from the reference program's by a relative error of at most 0.014.
Values may be sent and summed in bfloat16 or wider, within the bound.
A program may use at most 64 MiB of HBM per device.

```python
import math
import jax
import jax.numpy as jnp
from jax import lax

RADIAL = 512
VIBRATION = 8
ANGULAR = 1024
STEPS = 3
HELICITY = 4


def draw_kinetic(key, part):
    first = jax.random.fold_in(jax.random.fold_in(key, 17), 0)
    noise = jax.random.truncated_normal(first, -4.0, 4.0, (RADIAL, RADIAL), jnp.float32)
    sym = (noise + noise.T) * (0.5 / RADIAL ** 0.5)
    return jnp.clip(sym, -1.0, 1.0).astype(jnp.bfloat16)


def steps_of(own_key, dims, cuts, low, high):
    loudness = 1.0
    for axis_at, blocks in cuts:
        draws = jax.random.uniform(jax.random.fold_in(jax.random.fold_in(own_key, 6), axis_at), (blocks,), jnp.float32, low / len(cuts), high / len(cuts))
        loudness = loudness * jnp.repeat(jnp.exp(draws), dims[axis_at] // blocks).reshape((-1,) + (1,) * (len(dims) - 1 - axis_at))
    return loudness


def bell_draw(key, extent, width, reach, cuts=(), held_as=jnp.bfloat16):
    values = width * jax.random.normal(key, extent, jnp.float32)
    if cuts:
        values = values * steps_of(key, extent, cuts, -0.22, 0.18)
    return jnp.clip(values, -reach, reach).astype(held_as)


def setup_inputs(seed: int = 0) -> dict:
    streams_of = jax.random.split(jax.random.key(seed), 9)
    older_packet = bell_draw(streams_of[0], (HELICITY, RADIAL, VIBRATION, ANGULAR), 1.0, 6.0, ((0, 4), (1, 8)), jnp.float32)
    newer_packet = bell_draw(streams_of[1], (HELICITY, RADIAL, VIBRATION, ANGULAR), 1.0, 6.0, ((0, 4), (1, 8)), jnp.float32)
    kinetic = draw_kinetic(jax.random.fold_in(streams_of[8], 71), 0)
    transform = bell_draw(streams_of[3], (HELICITY, ANGULAR, ANGULAR), ANGULAR ** -0.5, 0.1875, ((0, 4),))
    potential = jnp.clip(jax.random.uniform(streams_of[4], (RADIAL, VIBRATION, ANGULAR), jnp.float32, -2.0, 2.0) * steps_of(streams_of[4], (RADIAL, VIBRATION, ANGULAR), ((0, 8),), -0.4, 0.0), -2.0, 2.0).astype(jnp.bfloat16)
    coupling = jnp.clip(jnp.exp(math.log(1.5) - 1.6133518 * jax.random.uniform(streams_of[5], (HELICITY, ANGULAR), jnp.float32) ** steps_of(streams_of[5], (HELICITY, ANGULAR), ((0, 4),), -0.2, 0.2)), 0.29882812, 1.5).astype(jnp.bfloat16)
    radial_weight = jnp.clip(jnp.exp(jax.random.uniform(streams_of[6], (RADIAL,), jnp.float32, math.log(0.3), math.log(2.0))), 0.3, 2.0)
    damping = jnp.clip(0.6 + 0.39999998 * jax.random.uniform(streams_of[7], (RADIAL,), jnp.float32) ** steps_of(streams_of[7], (RADIAL,), ((0, 8),), -0.2, 0.2), 0.6, 1.0)
    return {"older_packet": older_packet, "newer_packet": newer_packet, "kinetic": kinetic, "transform": transform, "potential": potential, "coupling": coupling, "radial_weight": radial_weight, "damping": damping}


SCALE_FACTOR = 0.35


def angular_block(rounded_block, matrix, potential_flat):
    flat = rounded_block.reshape(RADIAL * VIBRATION, ANGULAR)
    grid = jnp.dot(flat, matrix, preferred_element_type=jnp.float32)
    grid_values = (grid * potential_flat).astype(jnp.bfloat16)
    back = lax.dot_general(grid_values, matrix, (((1,), (1,)), ((), ())), preferred_element_type=jnp.float32)
    return back.reshape(RADIAL, VIBRATION, ANGULAR)


def reference(older_packet, newer_packet, kinetic, transform, potential, coupling, radial_weight, damping):
    kinetic_wide = kinetic.astype(jnp.float32)
    potential_flat = potential.astype(jnp.float32).reshape(RADIAL * VIBRATION, ANGULAR)
    coefficient = coupling.astype(jnp.float32)
    lower_coef = jnp.concatenate([jnp.zeros((1, ANGULAR), jnp.float32), coefficient[:-1]], axis=0)
    damp = damping[None, :, None, None]
    previous = older_packet
    current = newer_packet
    for _ in range(STEPS):
        rounded = current.astype(jnp.bfloat16)
        widened = rounded.astype(jnp.float32)
        radial_part = jnp.einsum("rs,ksva->krva", kinetic_wide, widened)
        empty = jnp.zeros((1, RADIAL, VIBRATION, ANGULAR), jnp.float32)
        below = jnp.concatenate([empty, widened[:-1]], axis=0)
        above = jnp.concatenate([widened[1:], empty], axis=0)
        coriolis_part = radial_weight[None, :, None, None] * (lower_coef[:, None, None, :] * below + coefficient[:, None, None, :] * above)
        off_grid = (radial_part + coriolis_part).astype(jnp.bfloat16)
        off_grid = lax.optimization_barrier(off_grid).astype(jnp.float32)
        angular_part = lax.map(lambda pair: angular_block(pair[0], pair[1], potential_flat), (rounded, transform))
        applied = SCALE_FACTOR * (off_grid + angular_part)
        following = damp * (2.0 * applied - damp * previous)
        previous = current
        current = following
    return previous, current
```

```python
import functools

import jax
import jax.numpy as jnp
from jax import lax
from jax.experimental import pallas as pl
from jax.experimental.pallas import tpu as pltpu
from jax.sharding import PartitionSpec as P

STEPS = 3


SCALE_FACTOR = 0.35
VMEM_LIMIT = 60 * 1024 * 1024 - 128 * 1024


def from_behind(array, axis, by):
    devices = lax.axis_size(axis)
    pairs = [(i, i + by) for i in range(devices) if 0 <= i + by < devices]
    return lax.ppermute(array, axis, pairs)


def coriolis_term(block, coefs, weights):
    lower_block, lower_coefs = from_behind((block, coefs), "hel", 1)
    upper_block = from_behind(block, "hel", -1)
    below = jnp.concatenate([lower_block, block[:-1]], axis=0).astype(jnp.float32)
    below_coefs = jnp.concatenate([lower_coefs, coefs[:-1]], axis=0).astype(jnp.float32)
    above = jnp.concatenate([block[1:], upper_block], axis=0).astype(jnp.float32)
    mixed = below_coefs[:, None, :] * below + coefs.astype(jnp.float32)[:, None, :] * above
    return weights[None, :, None] * mixed


def body(
    older_packet, newer_packet, kinetic, transform, potential, coupling, radial_weight, damping
):
    hel_rows, rad_rows, vib_count, ang_count = newer_packet.shape
    flat_width = vib_count * ang_count
    rank = lax.axis_index("rad")
    previous = older_packet.reshape(hel_rows, rad_rows, flat_width)
    current = newer_packet.reshape(hel_rows, rad_rows, flat_width)
    potential_flat = potential.astype(jnp.float32).reshape(1, rad_rows * vib_count, ang_count)
    tiled_coefs = jnp.tile(coupling, (1, vib_count))
    damp = damping[None, :, None]
    for _ in range(STEPS):
        rounded = current.astype(jnp.bfloat16)
        regrouped = lax.all_to_all(rounded, "rad", split_axis=2, concat_axis=1, tiled=True)
        kinetic_term = jnp.einsum(
            "rs,ksc->krc", kinetic, regrouped, preferred_element_type=jnp.float32
        )
        returned = lax.all_to_all(kinetic_term, "rad", split_axis=1, concat_axis=2, tiled=True)
        start = rank * rad_rows
        local_weights = lax.dynamic_slice_in_dim(radial_weight, start, rad_rows, 0)
        summed = returned + coriolis_term(rounded, tiled_coefs, local_weights)
        off_grid = summed.astype(jnp.bfloat16).astype(jnp.float32)
        angular_rows = rounded.reshape(hel_rows, rad_rows * vib_count, ang_count)
        grid = jnp.einsum(
            "kna,kag->kng", angular_rows, transform, preferred_element_type=jnp.float32
        )
        grid_values = (grid * potential_flat).astype(jnp.bfloat16)
        angular_part = jnp.einsum(
            "kng,kag->kna", grid_values, transform, preferred_element_type=jnp.float32
        )
        applied = SCALE_FACTOR * (off_grid + angular_part.reshape(hel_rows, rad_rows, flat_width))
        following = damp * (2.0 * applied - damp * previous)
        previous = current
        current = following
    shape = (hel_rows, rad_rows, vib_count, ang_count)
    return (previous.reshape(shape), current.reshape(shape))


def by_vibration(
    older_packet, newer_packet, kinetic, transform, potential, coupling, radial_weight, damping
):
    hel_rows, rad_rows, vib_count, ang_count = newer_packet.shape
    devices = lax.axis_size("rad")

    def scatter(array):
        return lax.all_to_all(array, "rad", split_axis=2, concat_axis=1, tiled=True)

    rounded = scatter(newer_packet.astype(jnp.bfloat16))
    previous = scatter(older_packet.astype(jnp.bfloat16)).astype(jnp.float32)
    pot = scatter(potential[None])[0].astype(jnp.float32)
    damp = lax.all_gather(damping, "rad", tiled=True)[None, :, None, None]
    weight = radial_weight[None, :, None, None]
    current = rounded.astype(jnp.float32)
    lower_coefs = from_behind(coupling, "hel", 1)
    coefs = jnp.concatenate([lower_coefs, coupling], axis=0).astype(jnp.float32)
    coefs = coefs[:, None, None, :]
    history = []
    for step in range(STEPS):
        lower = from_behind(rounded[-1:], "hel", 1)
        upper = from_behind(rounded[:1], "hel", -1)
        padded = jnp.concatenate([lower, rounded, upper], axis=0).astype(jnp.float32)
        mixed = coefs[:-1] * padded[:-2] + coefs[1:] * padded[2:]
        radial = jnp.einsum(
            "rs,ksva->krva", kinetic, rounded, preferred_element_type=jnp.float32
        )
        off_grid = radial + weight * mixed
        grid = jnp.einsum(
            "krva,kag->krvg", rounded, transform, preferred_element_type=jnp.float32
        )
        grid_values = (grid * pot[None]).astype(jnp.bfloat16)
        angular = jnp.einsum(
            "krvg,kag->krva", grid_values, transform, preferred_element_type=jnp.float32
        )
        applied = SCALE_FACTOR * (off_grid + angular)
        following = damp * (2.0 * applied - damp * previous)
        previous = current
        current = following
        rounded = current.astype(jnp.bfloat16)
        history.append(rounded)

    def gather(array):
        back = lax.all_to_all(array, "rad", split_axis=1, concat_axis=2, tiled=True)
        return back.astype(jnp.float32)

    return gather(history[-2]), gather(history[-1])


MESH = pl.DeviceIdType.MESH
POT, NEW, OLD, DAMP, OUT3, OUT4 = range(6)


def xor(a, b, n):
    bit, total = 1, 0
    while bit < n:
        total = total + bit * ((a // bit + b // bit) % 2)
        bit *= 2
    return total


def packet_kernel(
    n, hels,
    newer, older, kinetic, transform, potential, coupling, weight, damping,
    res3, res4,
    newer_v, older_v, kin, kin_of, tr, pot_in, pot_wide, coef, coef_low, damp_own, damp_all,
    weight_all, damp_col, weight_col, send_pot, send_new, send_old, pot, x0, x1, x2, x3, x4,
    total, second, grid, low, high, back3, back4,
    in_sem, lane_sem, rad_send, rad_recv, pot_send, pot_recv, hel_send, hel_recv, coef_sem,
):
    me = lax.axis_index("rad")
    hel = lax.axis_index("hel")
    rows = send_new.shape[1]
    ang = newer.shape[1]
    width = ang // hels
    half = n // 2
    far = half // 2
    near = half - far
    has_low = hel > 0
    has_high = hel < hels - 1

    def partner(i):
        return xor(me, (i + half) % n + (i + half) // n, n)

    def across(s):
        side = me // half
        return xor(me % half, s + side * (half - 1 - 2 * s), half)

    def block(c):
        return pl.ds(pl.multiple_of(c * rows, rows), rows)

    loads = [
        pltpu.make_async_copy(src, dst, in_sem.at[s])
        for s, (src, dst) in enumerate(
            (
                (potential.at[:, :, pl.ds(pl.multiple_of(hel * width, width), width)], pot_in),
                (damping, damp_own),
                (coupling, coef),
                (weight, weight_all),
                (kinetic, kin),
                (transform, tr),
            )
        )
    ]

    def lanes(l):
        return pl.ds(pl.multiple_of(l * 128, 128), 128)

    def newer_load(l):
        return pltpu.make_async_copy(newer.at[:, lanes(l)], newer_v.at[l], lane_sem.at[0, l])

    def older_load(l):
        return pltpu.make_async_copy(older.at[:, lanes(l)], older_v.at[l], lane_sem.at[1, l])

    def each_lane(copy, method):
        @pl.loop(0, ang // 128)
        def _(l):
            getattr(copy(l), method)()

    for load in loads[:3]:
        load.start()
    each_lane(newer_load, "start")
    each_lane(older_load, "start")
    for load in loads[3:]:
        load.start()

    barrier = pltpu.get_barrier_semaphore()

    @pl.loop(1, n)
    def _(j):
        pl.semaphore_signal(
            barrier, inc=1, device_id={"rad": lax.rem(me + j, n)}, device_id_type=MESH
        )

    @pl.loop(1, hels)
    def _(j):
        pl.semaphore_signal(
            barrier, inc=1, device_id={"hel": lax.rem(hel + j, hels)}, device_id_type=MESH
        )

    pl.semaphore_wait(barrier, n + hels - 2)

    def over_rad(kind, src, dst, i):
        return pltpu.make_async_remote_copy(
            src_ref=src,
            dst_ref=dst,
            send_sem=rad_send.at[kind, i],
            recv_sem=rad_recv.at[kind, i],
            device_id={"rad": partner(i)},
            device_id_type=MESH,
        )

    def pot_copy(i):
        return over_rad(POT, send_pot.at[i], pot.at[hel, block(me)], i)

    def new_copy(i):
        return over_rad(NEW, send_new.at[i], x1.at[block(me)], i)

    def old_copy(i):
        return over_rad(OLD, send_old.at[i], x0.at[block(me)], i)

    def damp_copy(i):
        return over_rad(DAMP, damp_own, damp_all.at[me], i)

    def out3_copy(i):
        return over_rad(OUT3, x3.at[block(partner(i))], back3.at[me], i)

    def out4_copy(i):
        return over_rad(OUT4, x4.at[block(partner(i))], back4.at[me], i)

    def pot_share(j):
        return pltpu.make_async_remote_copy(
            src_ref=pot.at[hel],
            dst_ref=pot.at[hel],
            send_sem=pot_send.at[j],
            recv_sem=pot_recv.at[j],
            device_id={"hel": lax.rem(hel + j, hels)},
            device_id_type=MESH,
        )

    coef_copy = pltpu.make_async_remote_copy(
        src_ref=coef,
        dst_ref=coef_low,
        send_sem=coef_sem.at[0],
        recv_sem=coef_sem.at[1],
        device_id={"hel": lax.rem(hel + 1, hels)},
        device_id_type=MESH,
    )

    def hel_up(step, x, c):
        return pltpu.make_async_remote_copy(
            src_ref=x.at[block(c)],
            dst_ref=low.at[step, block(c)],
            send_sem=hel_send.at[step, 0, c],
            recv_sem=hel_recv.at[step, 0, c],
            device_id={"hel": lax.rem(hel + 1, hels)},
            device_id_type=MESH,
        )

    def hel_down(step, x, c):
        return pltpu.make_async_remote_copy(
            src_ref=x.at[block(c)],
            dst_ref=high.at[step, block(c)],
            send_sem=hel_send.at[step, 1, c],
            recv_sem=hel_recv.at[step, 1, c],
            device_id={"hel": lax.rem(hel - 1 + hels, hels)},
            device_id_type=MESH,
        )

    def hel_start(step, x, c):
        @pl.when(has_high)
        def _():
            hel_up(step, x, c).start()

        @pl.when(has_low)
        def _():
            hel_down(step, x, c).start()

    def hel_wait_recv(step, x, c):
        @pl.when(has_low)
        def _():
            hel_up(step, x, c).wait_recv()

        @pl.when(has_high)
        def _():
            hel_down(step, x, c).wait_recv()

    def hel_wait_send(step, x, c):
        @pl.when(has_high)
        def _():
            hel_up(step, x, c).wait_send()

        @pl.when(has_low)
        def _():
            hel_down(step, x, c).wait_send()

    def trailing(make, copy):
        @pl.loop(0, n - 1)
        def _(i):
            make(i)

            @pl.when(i > 0)
            def _():
                copy(i - 1).start()

    everything = pl.ds(0, n * rows)

    loads[0].wait()
    for l in range(width // 128):
        part = pot_in[:, :, 128 * l : 128 * (l + 1)].astype(jnp.float32)
        pot_wide[l] = part.reshape(pot_wide.shape[1:])

    def picked(ref, c):
        return jnp.concatenate(
            [
                ref[l, pl.ds(c, rows, stride=n), :]
                for l in range(ref.shape[0])
            ],
            axis=1,
        ).astype(jnp.bfloat16)

    def make_pot(i):
        send_pot[i] = picked(pot_wide, partner(i))

    trailing(make_pot, pot_copy)
    pot[hel, block(me)] = picked(pot_wide, me)
    pot_copy(n - 2).start()

    each_lane(newer_load, "wait")

    def make_new(i):
        send_new[i] = picked(newer_v, partner(i))

    trailing(make_new, new_copy)
    x1[block(me)] = picked(newer_v, me)
    new_copy(n - 2).start()

    loads[1].wait()
    loads[2].wait()

    @pl.loop(0, n - 1)
    def _(i):
        damp_copy(i).start()

    @pl.when(has_high)
    def _():
        coef_copy.start()

    each_lane(older_load, "wait")

    def make_old(i):
        send_old[i] = picked(older_v, partner(i))

    trailing(make_old, old_copy)
    x0[block(me)] = picked(older_v, me)
    old_copy(n - 2).start()
    damp_all[me] = damp_own[...]

    @pl.when(jnp.logical_not(has_low))
    def _():
        low[...] = jnp.zeros_like(low)
        coef_low[...] = jnp.zeros_like(coef_low)

    @pl.when(jnp.logical_not(has_high))
    def _():
        high[...] = jnp.zeros_like(high)

    for load in loads[3:]:
        load.wait()

    for c in range(n):
        kin_of[c] = kin[:, c * rows : (c + 1) * rows]

    @pl.loop(0, n - 1)
    def _(i):
        pot_copy(i).wait_recv()

    @pl.loop(1, hels)
    def _(j):
        pot_share(j).start()

    @pl.loop(0, n - 1)
    def _(i):
        damp_copy(i).wait_recv()

    @pl.when(has_low)
    def _():
        coef_copy.wait_recv()

    line = lax.broadcasted_iota(jnp.int32, (rows, rows), 0)
    lane = lax.broadcasted_iota(jnp.int32, (rows, rows), 1)

    def column(row):
        diagonal = jnp.where(line == lane, jnp.broadcast_to(row, (rows, rows)), 0.0)
        return jnp.broadcast_to(jnp.sum(diagonal, axis=1, keepdims=True), (rows, 128))

    @pl.loop(0, n)
    def _(c):
        damp_col[block(c)] = column(damp_all[c])

    for c in range(n):
        part = weight_all[:, c * rows : (c + 1) * rows]
        weight_col[c * rows : (c + 1) * rows] = column(part)

    def near_side(visit):
        @pl.loop(half, n - 1)
        def _(i):
            visit(i)

    def far_side(first, last, visit):
        @pl.loop(first, last)
        def _(s):
            visit(across(s))

    hel_start(0, x1, me)

    def new_arrived(i):
        new_copy(i).wait_recv()
        hel_start(0, x1, partner(i))

    near_side(new_arrived)
    far_side(0, half, new_arrived)

    @pl.loop(1, hels)
    def _(j):
        pot_share(j).wait_recv()

    def to_grid(x, span):
        values = jnp.dot(x[span], tr[...], preferred_element_type=jnp.float32)
        for t in range(hels):
            part = values[:, t * width : (t + 1) * width] * pot[t, span].astype(jnp.float32)
            grid[span, t * width : (t + 1) * width] = part.astype(jnp.bfloat16)

    def from_grid(span):
        return lax.dot_general(
            grid[span], tr[...], (((1,), (1,)), ((), ())), preferred_element_type=jnp.float32
        )

    def multiply(x):
        to_grid(x, everything)
        radial = jnp.dot(kin[...], x[...], preferred_element_type=jnp.float32)
        total[...] = from_grid(everything) + radial

    lower_coef = coef_low[...].astype(jnp.float32)
    upper_coef = coef[...].astype(jnp.float32)

    def finish(step, whole, prev, c):
        span = block(c)
        damp = damp_col[span, 0:1]
        mixed = lower_coef * low[step, span].astype(jnp.float32)
        mixed = mixed + upper_coef * high[step, span].astype(jnp.float32)
        applied = SCALE_FACTOR * (whole + weight_col[span, 0:1] * mixed)
        following = damp * (2.0 * applied - damp * prev[span].astype(jnp.float32))
        return following.astype(jnp.bfloat16)

    multiply(x1)

    @pl.loop(0, n)
    def _(c):
        hel_wait_recv(0, x1, c)

    def advance(c):
        x2[block(c)] = finish(0, total[block(c)], x0, c)
        hel_start(1, x2, c)

    def spread(c):
        return jnp.dot(kin_of[c], x2[block(c)], preferred_element_type=jnp.float32)

    def turn(c):
        to_grid(x2, block(c))
        second[block(c)] += from_grid(block(c))

    advance(me)
    second[...] = spread(me)
    turn(me)

    def old_arrived(i):
        old_copy(i).wait_recv()
        advance(partner(i))
        second[...] += spread(partner(i))

    def old_turned(i):
        old_arrived(i)
        turn(partner(i))

    near_side(old_turned)
    far_side(0, near, old_turned)
    far_side(near, half - 1, old_arrived)
    last = across(half - 1)
    late = partner(last)
    old_copy(last).wait_recv()
    advance(late)

    def make3(i):
        c = partner(i)
        hel_wait_recv(1, x2, c)
        part = jnp.dot(
            kin_of[late, block(c)], x2[block(late)], preferred_element_type=jnp.float32
        )
        x3[block(c)] = finish(1, second[block(c)] + part, x1, c)
        out3_copy(i).start()
        hel_start(2, x3, c)

    far_side(0, near, make3)

    @pl.loop(near, half)
    def _(s):
        turn(partner(across(s)))

    far_side(near, half, make3)
    near_side(make3)
    hel_wait_recv(1, x2, me)
    part = jnp.dot(
        kin_of[late, block(me)], x2[block(late)], preferred_element_type=jnp.float32
    )
    x3[block(me)] = finish(1, second[block(me)] + part, x1, me)
    hel_start(2, x3, me)

    multiply(x3)

    def make4(c):
        hel_wait_recv(2, x3, c)
        x4[block(c)] = finish(2, total[block(c)], x2, c)

    def send4(i):
        make4(partner(i))
        out4_copy(i).start()

    far_side(0, half, send4)
    near_side(send4)
    make4(me)

    def interleave(res, piece, c):
        for l in range(ang // 128):
            res[l, pl.ds(c, rows, stride=n), :] = piece[:, l * 128 : (l + 1) * 128].astype(
                jnp.float32
            )

    interleave(res3, x3[block(me)], me)
    interleave(res4, x4[block(me)], me)

    def arrived3(i):
        out3_copy(i).wait_recv()
        interleave(res3, back3[partner(i)], partner(i))

    def arrived4(i):
        out4_copy(i).wait_recv()
        interleave(res4, back4[partner(i)], partner(i))

    for arrived in (arrived3, arrived4):
        near_side(arrived)
        far_side(0, half, arrived)

    @pl.loop(0, n - 1)
    def _(i):
        for copy in (pot_copy, new_copy, old_copy, damp_copy, out3_copy, out4_copy):
            copy(i).wait_send()

    @pl.loop(1, hels)
    def _(j):
        pot_share(j).wait_send()

    @pl.when(has_high)
    def _():
        coef_copy.wait_send()

    @pl.loop(0, n)
    def _(c):
        hel_wait_send(0, x1, c)
        hel_wait_send(1, x2, c)
        hel_wait_send(2, x3, c)


def place_kernel(res3, res4, out_old, out_new, sem):
    copies = [
        pltpu.make_async_copy(
            res.at[l], out.at[:, pl.ds(128 * l, 128)], sem.at[s, l]
        )
        for s, (res, out) in enumerate(((res3, out_old), (res4, out_new)))
        for l in range(res.shape[0])
    ]
    for copy in copies:
        copy.start()
    for copy in copies:
        copy.wait()


def one_vibration(
    older_packet, newer_packet, kinetic, transform, potential, coupling, radial_weight, damping
):
    _, rows, n, ang = newer_packet.shape
    hels = lax.axis_size("hel")
    width = ang // hels
    points = n * rows
    bf16, f32 = jnp.bfloat16, jnp.float32
    vector = pltpu.VMEM((points, ang), bf16)
    blocks = pltpu.VMEM((n, rows, ang), bf16)
    wide = pltpu.VMEM((points, ang), f32)
    flat = jax.ShapeDtypeStruct((points, ang), f32)
    anywhere = pl.BlockSpec(memory_space=pl.ANY)
    inside = pl.BlockSpec(memory_space=pltpu.VMEM)
    sem = pltpu.SemaphoreType.DMA
    groups = ang // 128
    result = pltpu.VMEM((groups, points, 128), f32)
    results = pl.pallas_call(
        functools.partial(packet_kernel, n, hels),
        out_shape=(result, result),
        in_specs=[anywhere] * 8,
        out_specs=(inside, inside),
        scratch_shapes=[
            pltpu.VMEM((groups, points, 128), f32),
            pltpu.VMEM((groups, points, 128), f32),
            pltpu.VMEM((points, points), bf16),
            pltpu.VMEM((n, points, rows), bf16),
            pltpu.VMEM((ang, ang), bf16),
            pltpu.VMEM((rows, n, width), bf16),
            pltpu.VMEM((width // 128, points, 128), f32),
            pltpu.VMEM((1, ang), bf16),
            pltpu.VMEM((1, ang), bf16),
            pltpu.VMEM((1, rows), f32),
            pltpu.VMEM((n, 1, rows), f32),
            pltpu.VMEM((1, points), f32),
            pltpu.VMEM((points, 128), f32),
            pltpu.VMEM((points, 128), f32),
            pltpu.VMEM((n, rows, width), bf16),
            blocks,
            blocks,
            pltpu.VMEM((hels, points, width), bf16),
            vector,
            vector,
            vector,
            vector,
            vector,
            wide,
            wide,
            vector,
            pltpu.VMEM((STEPS, points, ang), bf16),
            pltpu.VMEM((STEPS, points, ang), bf16),
            blocks,
            blocks,
            sem((6,)),
            sem((2, groups)),
            sem((6, n)),
            sem((6, n)),
            sem((hels,)),
            sem((hels,)),
            sem((STEPS, 2, n)),
            sem((STEPS, 2, n)),
            sem((2,)),
        ],
        compiler_params=pltpu.CompilerParams(
            collective_id=0, has_side_effects=True, vmem_limit_bytes=VMEM_LIMIT
        ),
    )(
        newer_packet.reshape(points, ang),
        older_packet.reshape(points, ang),
        kinetic,
        transform[0],
        potential,
        coupling,
        radial_weight.reshape(1, points),
        damping.reshape(1, rows),
    )
    outs = pl.pallas_call(
        place_kernel,
        out_shape=(flat, flat),
        in_specs=[inside] * 2,
        out_specs=(anywhere, anywhere),
        scratch_shapes=[sem((2, groups))],
        compiler_params=pltpu.CompilerParams(vmem_limit_bytes=4 * 1024 * 1024),
    )(*results)
    shape = newer_packet.shape
    return outs[0].reshape(shape), outs[1].reshape(shape)


def fits(packet):
    hel_rows, rows, vibs, ang = packet.shape
    hels = lax.axis_size("hel")
    return (
        STEPS == 3
        and hel_rows == 1
        and vibs == lax.axis_size("rad")
        and vibs > 1
        and vibs & (vibs - 1) == 0
        and hels > 1
        and rows % 16 == 0
        and ang % (hels * 128) == 0
        and rows * vibs <= 512
        and ang <= 1024
    )


def whole_body(older_packet, newer_packet, *rest):
    if fits(newer_packet):
        return one_vibration(older_packet, newer_packet, *rest)
    if newer_packet.shape[2] % lax.axis_size("rad") == 0:
        return by_vibration(older_packet, newer_packet, *rest)
    return body(older_packet, newer_packet, *rest)


def solution(mesh):
    return jax.shard_map(
        whole_body,
        mesh=mesh,
        in_specs=(
            P("hel", "rad", None, None),
            P("hel", "rad", None, None),
            P(),
            P("hel", None, None),
            P("rad", None, None),
            P("hel", None),
            P(),
            P("rad"),
        ),
        out_specs=(P("hel", "rad", None, None), P("hel", "rad", None, None)),
        check_vma=False,
    )
```

```python
import functools

import jax
import jax.numpy as jnp
from jax import lax
from jax.experimental import pallas as pl
from jax.experimental.pallas import tpu as pltpu
from jax.sharding import PartitionSpec as P

STEPS = 3


SCALE_FACTOR = 0.35
VMEM_LIMIT = 60 * 1024 * 1024 - 128 * 1024


def from_behind(array, axis, by):
    devices = lax.axis_size(axis)
    pairs = [(i, i + by) for i in range(devices) if 0 <= i + by < devices]
    return lax.ppermute(array, axis, pairs)


def coriolis_term(block, coefs, weights):
    lower_block, lower_coefs = from_behind((block, coefs), "hel", 1)
    upper_block = from_behind(block, "hel", -1)
    below = jnp.concatenate([lower_block, block[:-1]], axis=0).astype(jnp.float32)
    below_coefs = jnp.concatenate([lower_coefs, coefs[:-1]], axis=0).astype(jnp.float32)
    above = jnp.concatenate([block[1:], upper_block], axis=0).astype(jnp.float32)
    mixed = below_coefs[:, None, :] * below + coefs.astype(jnp.float32)[:, None, :] * above
    return weights[None, :, None] * mixed


def body(
    older_packet, newer_packet, kinetic, transform, potential, coupling, radial_weight, damping
):
    hel_rows, rad_rows, vib_count, ang_count = newer_packet.shape
    flat_width = vib_count * ang_count
    rank = lax.axis_index("rad")
    previous = older_packet.reshape(hel_rows, rad_rows, flat_width)
    current = newer_packet.reshape(hel_rows, rad_rows, flat_width)
    potential_flat = potential.astype(jnp.float32).reshape(1, rad_rows * vib_count, ang_count)
    tiled_coefs = jnp.tile(coupling, (1, vib_count))
    damp = damping[None, :, None]
    for _ in range(STEPS):
        rounded = current.astype(jnp.bfloat16)
        regrouped = lax.all_to_all(rounded, "rad", split_axis=2, concat_axis=1, tiled=True)
        kinetic_term = jnp.einsum(
            "rs,ksc->krc", kinetic, regrouped, preferred_element_type=jnp.float32
        )
        returned = lax.all_to_all(kinetic_term, "rad", split_axis=1, concat_axis=2, tiled=True)
        start = rank * rad_rows
        local_weights = lax.dynamic_slice_in_dim(radial_weight, start, rad_rows, 0)
        summed = returned + coriolis_term(rounded, tiled_coefs, local_weights)
        off_grid = summed.astype(jnp.bfloat16).astype(jnp.float32)
        angular_rows = rounded.reshape(hel_rows, rad_rows * vib_count, ang_count)
        grid = jnp.einsum(
            "kna,kag->kng", angular_rows, transform, preferred_element_type=jnp.float32
        )
        grid_values = (grid * potential_flat).astype(jnp.bfloat16)
        angular_part = jnp.einsum(
            "kng,kag->kna", grid_values, transform, preferred_element_type=jnp.float32
        )
        applied = SCALE_FACTOR * (off_grid + angular_part.reshape(hel_rows, rad_rows, flat_width))
        following = damp * (2.0 * applied - damp * previous)
        previous = current
        current = following
    shape = (hel_rows, rad_rows, vib_count, ang_count)
    return (previous.reshape(shape), current.reshape(shape))


def by_vibration(
    older_packet, newer_packet, kinetic, transform, potential, coupling, radial_weight, damping
):
    hel_rows, rad_rows, vib_count, ang_count = newer_packet.shape
    devices = lax.axis_size("rad")

    def scatter(array):
        return lax.all_to_all(array, "rad", split_axis=2, concat_axis=1, tiled=True)

    rounded = scatter(newer_packet.astype(jnp.bfloat16))
    previous = scatter(older_packet.astype(jnp.bfloat16)).astype(jnp.float32)
    pot = scatter(potential[None])[0].astype(jnp.float32)
    damp = lax.all_gather(damping, "rad", tiled=True)[None, :, None, None]
    weight = radial_weight[None, :, None, None]
    current = rounded.astype(jnp.float32)
    lower_coefs = from_behind(coupling, "hel", 1)
    coefs = jnp.concatenate([lower_coefs, coupling], axis=0).astype(jnp.float32)
    coefs = coefs[:, None, None, :]
    history = []
    for step in range(STEPS):
        lower = from_behind(rounded[-1:], "hel", 1)
        upper = from_behind(rounded[:1], "hel", -1)
        padded = jnp.concatenate([lower, rounded, upper], axis=0).astype(jnp.float32)
        mixed = coefs[:-1] * padded[:-2] + coefs[1:] * padded[2:]
        radial = jnp.einsum(
            "rs,ksva->krva", kinetic, rounded, preferred_element_type=jnp.float32
        )
        off_grid = radial + weight * mixed
        grid = jnp.einsum(
            "krva,kag->krvg", rounded, transform, preferred_element_type=jnp.float32
        )
        grid_values = (grid * pot[None]).astype(jnp.bfloat16)
        angular = jnp.einsum(
            "krvg,kag->krva", grid_values, transform, preferred_element_type=jnp.float32
        )
        applied = SCALE_FACTOR * (off_grid + angular)
        following = damp * (2.0 * applied - damp * previous)
        previous = current
        current = following
        rounded = current.astype(jnp.bfloat16)
        history.append(rounded)

    def gather(array):
        back = lax.all_to_all(array, "rad", split_axis=1, concat_axis=2, tiled=True)
        return back.astype(jnp.float32)

    return gather(history[-2]), gather(history[-1])


MESH = pl.DeviceIdType.MESH
POT, NEW, OLD, DAMP, OUT3, OUT4 = range(6)


def xor(a, b, n):
    bit, total = 1, 0
    while bit < n:
        total = total + bit * ((a // bit + b // bit) % 2)
        bit *= 2
    return total


def packet_kernel(
    n, hels,
    newer, older, kinetic, transform, potential, coupling, weight, damping,
    res3, res4,
    newer_v, older_v, kin, tr, pot_in, pot_full, pot_wide, coef, coef_low, damp_own, damp_all,
    weight_all, damp_col, weight_col, send_pot, pot_mine, mine0, mine1, pot, x0, x1, x2, x3, x4,
    total, second, grid, low, high, back3, back4,
    in_sem, lane_sem, rad_send, rad_recv, pot_send, pot_recv, hel_send, hel_recv, coef_sem,
):
    me = lax.axis_index("rad")
    hel = lax.axis_index("hel")
    rows = send_pot.shape[1]
    ang = newer.shape[1]
    width = ang // hels
    half = n // 2
    far = half // 2
    near = half - far
    side = me // half
    has_low = hel > 0
    has_high = hel < hels - 1

    def partner(i):
        return xor(me, (i + half) % n + (i + half) // n, n)

    def across(s):
        return xor(me % half, s + side * (half - 1 - 2 * s), half)

    def block(c):
        return pl.ds(pl.multiple_of(c * rows, rows), rows)

    loads = [
        pltpu.make_async_copy(src, dst, in_sem.at[s])
        for s, (src, dst) in enumerate(
            (
                (potential.at[:, :, pl.ds(pl.multiple_of(hel * width, width), width)], pot_in),
                (damping, damp_own),
                (coupling, coef),
                (weight, weight_all),
                (transform, tr),
                (potential, pot_full),
                (kinetic, kin),
            )
        )
    ]

    def lanes(l):
        return pl.ds(pl.multiple_of(l * 128, 128), 128)

    def newer_load(l):
        return pltpu.make_async_copy(newer.at[:, lanes(l)], newer_v.at[l], lane_sem.at[0, l])

    def older_load(l):
        return pltpu.make_async_copy(older.at[:, lanes(l)], older_v.at[l], lane_sem.at[1, l])

    def each_lane(copy, method):
        @pl.loop(0, ang // 128)
        def _(l):
            getattr(copy(l), method)()

    for load in loads[:3]:
        load.start()
    each_lane(newer_load, "start")
    each_lane(older_load, "start")
    for load in loads[3:]:
        load.start()

    barrier = pltpu.get_barrier_semaphore()

    @pl.loop(1, n)
    def _(j):
        pl.semaphore_signal(
            barrier, inc=1, device_id={"rad": lax.rem(me + j, n)}, device_id_type=MESH
        )

    @pl.loop(1, hels)
    def _(j):
        pl.semaphore_signal(
            barrier, inc=1, device_id={"hel": lax.rem(hel + j, hels)}, device_id_type=MESH
        )

    pl.semaphore_wait(barrier, n + hels - 2)

    def over_rad(kind, src, dst, i):
        return pltpu.make_async_remote_copy(
            src_ref=src,
            dst_ref=dst,
            send_sem=rad_send.at[kind, i],
            recv_sem=rad_recv.at[kind, i],
            device_id={"rad": partner(i)},
            device_id_type=MESH,
        )

    def pot_copy(i):
        return over_rad(POT, send_pot.at[i], pot.at[hel, block(me)], i)

    def new_copy(i):
        return over_rad(NEW, mine1.at[block(partner(i))], x1.at[block(me)], i)

    def old_copy(i):
        return over_rad(OLD, mine0.at[block(partner(i))], x0.at[block(me)], i)

    def damp_copy(i):
        return over_rad(DAMP, damp_own, damp_all.at[me], i)

    def out3_copy(i):
        return over_rad(OUT3, x3.at[block(partner(i))], back3.at[me], i)

    def out4_copy(i):
        return over_rad(OUT4, x4.at[block(partner(i))], back4.at[me], i)

    def pot_share(j):
        return pltpu.make_async_remote_copy(
            src_ref=pot.at[hel],
            dst_ref=pot.at[hel],
            send_sem=pot_send.at[j],
            recv_sem=pot_recv.at[j],
            device_id={"hel": lax.rem(hel + j, hels)},
            device_id_type=MESH,
        )

    coef_copy = pltpu.make_async_remote_copy(
        src_ref=coef,
        dst_ref=coef_low,
        send_sem=coef_sem.at[0],
        recv_sem=coef_sem.at[1],
        device_id={"hel": lax.rem(hel + 1, hels)},
        device_id_type=MESH,
    )

    def hel_up(step, x, c):
        return pltpu.make_async_remote_copy(
            src_ref=x.at[block(c)],
            dst_ref=low.at[step, block(c)],
            send_sem=hel_send.at[step, 0, c],
            recv_sem=hel_recv.at[step, 0, c],
            device_id={"hel": lax.rem(hel + 1, hels)},
            device_id_type=MESH,
        )

    def hel_down(step, x, c):
        return pltpu.make_async_remote_copy(
            src_ref=x.at[block(c)],
            dst_ref=high.at[step, block(c)],
            send_sem=hel_send.at[step, 1, c],
            recv_sem=hel_recv.at[step, 1, c],
            device_id={"hel": lax.rem(hel - 1 + hels, hels)},
            device_id_type=MESH,
        )

    def hel_start(step, x, c):
        @pl.when(has_high)
        def _():
            hel_up(step, x, c).start()

        @pl.when(has_low)
        def _():
            hel_down(step, x, c).start()

    def hel_wait_recv(step, x, c):
        @pl.when(has_low)
        def _():
            hel_up(step, x, c).wait_recv()

        @pl.when(has_high)
        def _():
            hel_down(step, x, c).wait_recv()

    def hel_wait_send(step, x, c):
        @pl.when(has_high)
        def _():
            hel_up(step, x, c).wait_send()

        @pl.when(has_low)
        def _():
            hel_down(step, x, c).wait_send()

    def trailing(make, copy):
        @pl.loop(0, n - 1)
        def _(i):
            make(i)

            @pl.when(i > 0)
            def _():
                copy(i - 1).start()

    loads[0].wait()
    for l in range(width // 128):
        part = pot_in[:, :, 128 * l : 128 * (l + 1)].astype(jnp.float32)
        pot_wide[l] = part.reshape(pot_wide.shape[1:])

    def picked(ref, c, count):
        return jnp.concatenate(
            [ref[l, pl.ds(c, rows, stride=n), :] for l in range(count)], axis=1
        )

    def make_pot(i):
        send_pot[i] = picked(pot_wide, partner(i), width // 128).astype(jnp.bfloat16)

    trailing(make_pot, pot_copy)
    pot[hel, block(me)] = picked(pot_wide, me, width // 128).astype(jnp.bfloat16)
    pot_copy(n - 2).start()

    each_lane(newer_load, "wait")

    def make_new(i):
        mine1[block(partner(i))] = picked(newer_v, partner(i), ang // 128).astype(jnp.bfloat16)

    trailing(make_new, new_copy)
    mine1[block(me)] = picked(newer_v, me, ang // 128).astype(jnp.bfloat16)
    new_copy(n - 2).start()

    @pl.loop(0, n)
    def _(c):
        hel_start(0, mine1, c)

    x1[block(me)] = mine1[block(me)]
    loads[1].wait()
    loads[2].wait()

    @pl.loop(0, n - 1)
    def _(i):
        damp_copy(i).start()

    @pl.when(has_high)
    def _():
        coef_copy.start()

    damp_all[me] = damp_own[...]

    @pl.when(jnp.logical_not(has_low))
    def _():
        low[...] = jnp.zeros_like(low)
        coef_low[...] = jnp.zeros_like(coef_low)

    @pl.when(jnp.logical_not(has_high))
    def _():
        high[...] = jnp.zeros_like(high)

    line = lax.broadcasted_iota(jnp.int32, (rows, rows), 0)
    lane = lax.broadcasted_iota(jnp.int32, (rows, rows), 1)

    def column(row):
        diagonal = jnp.where(line == lane, jnp.broadcast_to(row, (rows, rows)), 0.0)
        return jnp.broadcast_to(jnp.sum(diagonal, axis=1, keepdims=True), (rows, 128))

    damp_col[block(me)] = column(damp_own[...])
    loads[3].wait()
    for c in range(n):
        part = weight_all[:, c * rows : (c + 1) * rows]
        weight_col[c * rows : (c + 1) * rows] = column(part)

    loads[4].wait()
    loads[5].wait()
    for l in range(ang // 128):
        part = pot_full[:, :, 128 * l : 128 * (l + 1)].astype(jnp.float32)
        pot_wide[l] = part.reshape(pot_wide.shape[1:])

    @pl.loop(0, n)
    def _(c):
        pot_mine[block(c)] = picked(pot_wide, c, ang // 128).astype(jnp.bfloat16)

    everything = pl.ds(0, n * rows)

    def from_grid(span):
        return lax.dot_general(
            grid[span], tr[...], (((1,), (1,)), ((), ())), preferred_element_type=jnp.float32
        )

    values = jnp.dot(mine1[...], tr[...], preferred_element_type=jnp.float32)
    grid[...] = (values * pot_mine[...].astype(jnp.float32)).astype(jnp.bfloat16)
    total[...] = from_grid(everything)

    @pl.loop(0, n - 1)
    def _(i):
        pot_copy(i).wait_recv()

    @pl.loop(1, hels)
    def _(j):
        pot_share(j).start()

    @pl.when(has_low)
    def _():
        coef_copy.wait_recv()

    lower_coef = coef_low[...].astype(jnp.float32)
    upper_coef = coef[...].astype(jnp.float32)

    def mixed(step, span):
        below = lower_coef * low[step, span].astype(jnp.float32)
        return below + upper_coef * high[step, span].astype(jnp.float32)

    each_lane(older_load, "wait")
    my_damp = damp_col[block(me), 0:1]
    my_weight = weight_col[block(me), 0:1]

    def make_old(c):
        hel_wait_recv(0, mine1, c)
        applied = SCALE_FACTOR * (total[block(c)] + my_weight * mixed(0, block(c)))
        prev = picked(older_v, c, ang // 128)
        mine0[block(c)] = (my_damp * (2.0 * applied - my_damp * prev)).astype(jnp.bfloat16)

    def send_old(i):
        make_old(partner(i))

    trailing(send_old, old_copy)
    old_copy(n - 2).start()
    make_old(me)
    x0[block(me)] = mine0[block(me)]

    @pl.loop(0, n - 1)
    def _(i):
        damp_copy(i).wait_recv()

    @pl.loop(0, n)
    def _(c):
        damp_col[block(c)] = column(damp_all[c])

    def near_side(visit):
        @pl.loop(half, n - 1)
        def _(i):
            visit(i)

    def far_side(first, last, visit):
        @pl.loop(first, last)
        def _(s):
            visit(across(s))

    loads[6].wait()

    @pl.loop(0, n - 1)
    def _(i):
        new_copy(i).wait_recv()

    total[...] = jnp.dot(kin[...], x1[...], preferred_element_type=jnp.float32)

    @pl.loop(1, hels)
    def _(j):
        pot_share(j).wait_recv()

    def to_grid(x, span):
        values = jnp.dot(x[span], tr[...], preferred_element_type=jnp.float32)
        for t in range(hels):
            part = values[:, t * width : (t + 1) * width] * pot[t, span].astype(jnp.float32)
            grid[span, t * width : (t + 1) * width] = part.astype(jnp.bfloat16)

    def multiply(x):
        to_grid(x, everything)
        radial = jnp.dot(kin[...], x[...], preferred_element_type=jnp.float32)
        total[...] = from_grid(everything) + radial

    def finish(step, whole, prev, c):
        span = block(c)
        damp = damp_col[span, 0:1]
        applied = SCALE_FACTOR * (whole + weight_col[span, 0:1] * mixed(step, span))
        following = damp * (2.0 * applied - damp * prev[span].astype(jnp.float32))
        return following.astype(jnp.bfloat16)

    def advance(c):
        span = block(c)
        scale = 2.0 * SCALE_FACTOR * damp_col[span, 0:1]
        x2[span] = (scale * total[span] + x0[span].astype(jnp.float32)).astype(jnp.bfloat16)
        hel_start(1, x2, c)

    def stretch(first, count):
        return pl.ds(pl.multiple_of(first * rows, count * rows), count * rows)

    ours = stretch(side * half, half)
    early = stretch((1 - side) * (half + near), far)
    late = stretch(half - side * near, near)

    def spread(to, source):
        return jnp.dot(kin[to, source], x2[source], preferred_element_type=jnp.float32)

    def turn(span):
        to_grid(x2, span)
        second[span] += from_grid(span)

    def old_arrived(i):
        old_copy(i).wait_recv()
        advance(partner(i))

    advance(me)
    near_side(old_arrived)
    second[...] = spread(everything, ours)
    turn(ours)
    far_side(near, half, old_arrived)
    second[...] += spread(everything, early)
    turn(early)
    far_side(0, near, old_arrived)

    def make3(c):
        hel_wait_recv(1, x2, c)
        x3[block(c)] = finish(1, second[block(c)], x1, c)

    def send3(i):
        make3(partner(i))
        out3_copy(i).start()
        hel_start(2, x3, partner(i))

    second[early] += spread(early, late)
    far_side(near, half, send3)
    second[late] += spread(late, late)
    second[ours] += spread(ours, late)
    turn(late)
    far_side(0, near, send3)
    near_side(send3)
    make3(me)
    hel_start(2, x3, me)

    multiply(x3)

    def make4(c):
        hel_wait_recv(2, x3, c)
        x4[block(c)] = finish(2, total[block(c)], x2, c)

    def send4(i):
        make4(partner(i))
        out4_copy(i).start()

    far_side(0, half, send4)
    near_side(send4)
    make4(me)

    def interleave(res, piece, c):
        for l in range(ang // 128):
            res[l, pl.ds(c, rows, stride=n), :] = piece[:, l * 128 : (l + 1) * 128].astype(
                jnp.float32
            )

    interleave(res3, x3[block(me)], me)
    interleave(res4, x4[block(me)], me)

    def arrived3(i):
        out3_copy(i).wait_recv()
        interleave(res3, back3[partner(i)], partner(i))

    def arrived4(i):
        out4_copy(i).wait_recv()
        interleave(res4, back4[partner(i)], partner(i))

    for arrived in (arrived3, arrived4):
        near_side(arrived)
        far_side(0, half, arrived)

    @pl.loop(0, n - 1)
    def _(i):
        for copy in (pot_copy, new_copy, old_copy, damp_copy, out3_copy, out4_copy):
            copy(i).wait_send()

    @pl.loop(1, hels)
    def _(j):
        pot_share(j).wait_send()

    @pl.when(has_high)
    def _():
        coef_copy.wait_send()

    @pl.loop(0, n)
    def _(c):
        hel_wait_send(0, mine1, c)
        hel_wait_send(1, x2, c)
        hel_wait_send(2, x3, c)


def place_kernel(res3, res4, out_old, out_new, sem):
    copies = [
        pltpu.make_async_copy(
            res.at[l], out.at[:, pl.ds(128 * l, 128)], sem.at[s, l]
        )
        for s, (res, out) in enumerate(((res3, out_old), (res4, out_new)))
        for l in range(res.shape[0])
    ]
    for copy in copies:
        copy.start()
    for copy in copies:
        copy.wait()


def one_vibration(
    older_packet, newer_packet, kinetic, transform, potential, coupling, radial_weight, damping
):
    _, rows, n, ang = newer_packet.shape
    hels = lax.axis_size("hel")
    width = ang // hels
    points = n * rows
    bf16, f32 = jnp.bfloat16, jnp.float32
    vector = pltpu.VMEM((points, ang), bf16)
    blocks = pltpu.VMEM((n, rows, ang), bf16)
    wide = pltpu.VMEM((points, ang), f32)
    flat = jax.ShapeDtypeStruct((points, ang), f32)
    anywhere = pl.BlockSpec(memory_space=pl.ANY)
    inside = pl.BlockSpec(memory_space=pltpu.VMEM)
    sem = pltpu.SemaphoreType.DMA
    groups = ang // 128
    result = pltpu.VMEM((groups, points, 128), f32)
    results = pl.pallas_call(
        functools.partial(packet_kernel, n, hels),
        out_shape=(result, result),
        in_specs=[anywhere] * 8,
        out_specs=(inside, inside),
        scratch_shapes=[
            pltpu.VMEM((groups, points, 128), f32),
            pltpu.VMEM((groups, points, 128), f32),
            pltpu.VMEM((points, points), bf16),
            pltpu.VMEM((ang, ang), bf16),
            pltpu.VMEM((rows, n, width), bf16),
            pltpu.VMEM((rows, n, ang), bf16),
            pltpu.VMEM((groups, points, 128), f32),
            pltpu.VMEM((1, ang), bf16),
            pltpu.VMEM((1, ang), bf16),
            pltpu.VMEM((1, rows), f32),
            pltpu.VMEM((n, 1, rows), f32),
            pltpu.VMEM((1, points), f32),
            pltpu.VMEM((points, 128), f32),
            pltpu.VMEM((points, 128), f32),
            pltpu.VMEM((n, rows, width), bf16),
            vector,
            vector,
            vector,
            pltpu.VMEM((hels, points, width), bf16),
            vector,
            vector,
            vector,
            vector,
            vector,
            wide,
            wide,
            vector,
            pltpu.VMEM((STEPS, points, ang), bf16),
            pltpu.VMEM((STEPS, points, ang), bf16),
            blocks,
            blocks,
            sem((7,)),
            sem((2, groups)),
            sem((6, n)),
            sem((6, n)),
            sem((hels,)),
            sem((hels,)),
            sem((STEPS, 2, n)),
            sem((STEPS, 2, n)),
            sem((2,)),
        ],
        compiler_params=pltpu.CompilerParams(
            collective_id=0, has_side_effects=True, vmem_limit_bytes=VMEM_LIMIT
        ),
    )(
        newer_packet.reshape(points, ang),
        older_packet.reshape(points, ang),
        kinetic,
        transform[0],
        potential,
        coupling,
        radial_weight.reshape(1, points),
        damping.reshape(1, rows),
    )
    outs = pl.pallas_call(
        place_kernel,
        out_shape=(flat, flat),
        in_specs=[inside] * 2,
        out_specs=(anywhere, anywhere),
        scratch_shapes=[sem((2, groups))],
        compiler_params=pltpu.CompilerParams(vmem_limit_bytes=4 * 1024 * 1024),
    )(*results)
    shape = newer_packet.shape
    return outs[0].reshape(shape), outs[1].reshape(shape)


def fits(packet):
    hel_rows, rows, vibs, ang = packet.shape
    hels = lax.axis_size("hel")
    return (
        STEPS == 3
        and hel_rows == 1
        and vibs == lax.axis_size("rad")
        and vibs > 1
        and vibs & (vibs - 1) == 0
        and vibs >= 4
        and rows * vibs % 512 == 0
        and hels > 1
        and rows % 16 == 0
        and ang % (hels * 128) == 0
        and rows * vibs <= 512
        and ang <= 1024
    )


def whole_body(older_packet, newer_packet, *rest):
    if fits(newer_packet):
        return one_vibration(older_packet, newer_packet, *rest)
    if newer_packet.shape[2] % lax.axis_size("rad") == 0:
        return by_vibration(older_packet, newer_packet, *rest)
    return body(older_packet, newer_packet, *rest)


def solution(mesh):
    return jax.shard_map(
        whole_body,
        mesh=mesh,
        in_specs=(
            P("hel", "rad", None, None),
            P("hel", "rad", None, None),
            P(),
            P("hel", None, None),
            P("rad", None, None),
            P("hel", None),
            P(),
            P("rad"),
        ),
        out_specs=(P("hel", "rad", None, None), P("hel", "rad", None, None)),
        check_vma=False,
    )
```

```python
import functools

import jax
import jax.numpy as jnp
from jax import lax
from jax.experimental import pallas as pl
from jax.experimental.pallas import tpu as pltpu
from jax.sharding import PartitionSpec as P

STEPS = 3


SCALE_FACTOR = 0.35
VMEM_LIMIT = 60 * 1024 * 1024 - 128 * 1024


def from_behind(array, axis, by):
    devices = lax.axis_size(axis)
    pairs = [(i, i + by) for i in range(devices) if 0 <= i + by < devices]
    return lax.ppermute(array, axis, pairs)


def coriolis_term(block, coefs, weights):
    lower_block, lower_coefs = from_behind((block, coefs), "hel", 1)
    upper_block = from_behind(block, "hel", -1)
    below = jnp.concatenate([lower_block, block[:-1]], axis=0).astype(jnp.float32)
    below_coefs = jnp.concatenate([lower_coefs, coefs[:-1]], axis=0).astype(jnp.float32)
    above = jnp.concatenate([block[1:], upper_block], axis=0).astype(jnp.float32)
    mixed = below_coefs[:, None, :] * below + coefs.astype(jnp.float32)[:, None, :] * above
    return weights[None, :, None] * mixed


def body(
    older_packet, newer_packet, kinetic, transform, potential, coupling, radial_weight, damping
):
    hel_rows, rad_rows, vib_count, ang_count = newer_packet.shape
    flat_width = vib_count * ang_count
    rank = lax.axis_index("rad")
    previous = older_packet.reshape(hel_rows, rad_rows, flat_width)
    current = newer_packet.reshape(hel_rows, rad_rows, flat_width)
    potential_flat = potential.astype(jnp.float32).reshape(1, rad_rows * vib_count, ang_count)
    tiled_coefs = jnp.tile(coupling, (1, vib_count))
    damp = damping[None, :, None]
    for _ in range(STEPS):
        rounded = current.astype(jnp.bfloat16)
        regrouped = lax.all_to_all(rounded, "rad", split_axis=2, concat_axis=1, tiled=True)
        kinetic_term = jnp.einsum(
            "rs,ksc->krc", kinetic, regrouped, preferred_element_type=jnp.float32
        )
        returned = lax.all_to_all(kinetic_term, "rad", split_axis=1, concat_axis=2, tiled=True)
        start = rank * rad_rows
        local_weights = lax.dynamic_slice_in_dim(radial_weight, start, rad_rows, 0)
        summed = returned + coriolis_term(rounded, tiled_coefs, local_weights)
        off_grid = summed.astype(jnp.bfloat16).astype(jnp.float32)
        angular_rows = rounded.reshape(hel_rows, rad_rows * vib_count, ang_count)
        grid = jnp.einsum(
            "kna,kag->kng", angular_rows, transform, preferred_element_type=jnp.float32
        )
        grid_values = (grid * potential_flat).astype(jnp.bfloat16)
        angular_part = jnp.einsum(
            "kng,kag->kna", grid_values, transform, preferred_element_type=jnp.float32
        )
        applied = SCALE_FACTOR * (off_grid + angular_part.reshape(hel_rows, rad_rows, flat_width))
        following = damp * (2.0 * applied - damp * previous)
        previous = current
        current = following
    shape = (hel_rows, rad_rows, vib_count, ang_count)
    return (previous.reshape(shape), current.reshape(shape))


def by_vibration(
    older_packet, newer_packet, kinetic, transform, potential, coupling, radial_weight, damping
):
    hel_rows, rad_rows, vib_count, ang_count = newer_packet.shape
    devices = lax.axis_size("rad")

    def scatter(array):
        return lax.all_to_all(array, "rad", split_axis=2, concat_axis=1, tiled=True)

    rounded = scatter(newer_packet.astype(jnp.bfloat16))
    previous = scatter(older_packet.astype(jnp.bfloat16)).astype(jnp.float32)
    pot = scatter(potential[None])[0].astype(jnp.float32)
    damp = lax.all_gather(damping, "rad", tiled=True)[None, :, None, None]
    weight = radial_weight[None, :, None, None]
    current = rounded.astype(jnp.float32)
    lower_coefs = from_behind(coupling, "hel", 1)
    coefs = jnp.concatenate([lower_coefs, coupling], axis=0).astype(jnp.float32)
    coefs = coefs[:, None, None, :]
    history = []
    for step in range(STEPS):
        lower = from_behind(rounded[-1:], "hel", 1)
        upper = from_behind(rounded[:1], "hel", -1)
        padded = jnp.concatenate([lower, rounded, upper], axis=0).astype(jnp.float32)
        mixed = coefs[:-1] * padded[:-2] + coefs[1:] * padded[2:]
        radial = jnp.einsum(
            "rs,ksva->krva", kinetic, rounded, preferred_element_type=jnp.float32
        )
        off_grid = radial + weight * mixed
        grid = jnp.einsum(
            "krva,kag->krvg", rounded, transform, preferred_element_type=jnp.float32
        )
        grid_values = (grid * pot[None]).astype(jnp.bfloat16)
        angular = jnp.einsum(
            "krvg,kag->krva", grid_values, transform, preferred_element_type=jnp.float32
        )
        applied = SCALE_FACTOR * (off_grid + angular)
        following = damp * (2.0 * applied - damp * previous)
        previous = current
        current = following
        rounded = current.astype(jnp.bfloat16)
        history.append(rounded)

    def gather(array):
        back = lax.all_to_all(array, "rad", split_axis=1, concat_axis=2, tiled=True)
        return back.astype(jnp.float32)

    return gather(history[-2]), gather(history[-1])


MESH = pl.DeviceIdType.MESH
POT, NEW, OLD, DAMP, OUT3, OUT4 = range(6)


def xor(a, b, n):
    bit, total = 1, 0
    while bit < n:
        total = total + bit * ((a // bit + b // bit) % 2)
        bit *= 2
    return total


def packet_kernel(
    n, hels,
    newer, older, kinetic, transform, potential, coupling, weight, damping,
    res3, res4,
    newer_v, older_v, kin, tr, pot_in, pot_full, pot_wide, coef, coef_low, damp_own, damp_all,
    weight_all, damp_col, weight_col, send_pot, pot_mine, mine0, mine1, pot, x0, x1, x2, x3, x4,
    total, second, grid, low, high, back3, back4,
    in_sem, lane_sem, rad_send, rad_recv, pot_send, pot_recv, hel_send, hel_recv, coef_sem,
):
    me = lax.axis_index("rad")
    hel = lax.axis_index("hel")
    rows = send_pot.shape[1]
    ang = newer.shape[1]
    width = ang // hels
    half = n // 2
    far = half // 2
    near = half - far
    side = me // half
    has_low = hel > 0
    has_high = hel < hels - 1

    def partner(i):
        odd = i % 2
        return xor(me, odd * ((i + 1) // 2) + (1 - odd) * (half + i // 2), n)

    def across(s):
        return 2 * xor(me % half, s + side * (half - 1 - 2 * s), half)

    def block(c):
        return pl.ds(pl.multiple_of(c * rows, rows), rows)

    loads = [
        pltpu.make_async_copy(src, dst, in_sem.at[s])
        for s, (src, dst) in enumerate(
            (
                (potential.at[:, :, pl.ds(pl.multiple_of(hel * width, width), width)], pot_in),
                (damping, damp_own),
                (coupling, coef),
                (weight, weight_all),
                (transform, tr),
                (potential, pot_full),
                (kinetic, kin),
            )
        )
    ]

    def lanes(l):
        return pl.ds(pl.multiple_of(l * 128, 128), 128)

    def newer_load(l):
        return pltpu.make_async_copy(newer.at[:, lanes(l)], newer_v.at[l], lane_sem.at[0, l])

    def older_load(l):
        return pltpu.make_async_copy(older.at[:, lanes(l)], older_v.at[l], lane_sem.at[1, l])

    def each_lane(copy, method):
        @pl.loop(0, ang // 128)
        def _(l):
            getattr(copy(l), method)()

    for load in loads[:3]:
        load.start()
    each_lane(newer_load, "start")
    each_lane(older_load, "start")
    for load in loads[3:]:
        load.start()

    barrier = pltpu.get_barrier_semaphore()

    @pl.loop(1, n)
    def _(j):
        pl.semaphore_signal(
            barrier, inc=1, device_id={"rad": lax.rem(me + j, n)}, device_id_type=MESH
        )

    @pl.loop(1, hels)
    def _(j):
        pl.semaphore_signal(
            barrier, inc=1, device_id={"hel": lax.rem(hel + j, hels)}, device_id_type=MESH
        )

    pl.semaphore_wait(barrier, n + hels - 2)

    def over_rad(kind, src, dst, i):
        return pltpu.make_async_remote_copy(
            src_ref=src,
            dst_ref=dst,
            send_sem=rad_send.at[kind, i],
            recv_sem=rad_recv.at[kind, i],
            device_id={"rad": partner(i)},
            device_id_type=MESH,
        )

    def pot_copy(i):
        return over_rad(POT, send_pot.at[i], pot.at[hel, block(me)], i)

    def new_copy(i):
        return over_rad(NEW, mine1.at[block(partner(i))], x1.at[block(me)], i)

    def old_copy(i):
        return over_rad(OLD, mine0.at[block(partner(i))], x0.at[block(me)], i)

    def damp_copy(i):
        return over_rad(DAMP, damp_own, damp_all.at[me], i)

    def out3_copy(i):
        return over_rad(OUT3, x3.at[block(partner(i))], back3.at[me], i)

    def out4_copy(i):
        return over_rad(OUT4, x4.at[block(partner(i))], back4.at[me], i)

    def pot_share(j):
        return pltpu.make_async_remote_copy(
            src_ref=pot.at[hel],
            dst_ref=pot.at[hel],
            send_sem=pot_send.at[j],
            recv_sem=pot_recv.at[j],
            device_id={"hel": lax.rem(hel + j, hels)},
            device_id_type=MESH,
        )

    coef_copy = pltpu.make_async_remote_copy(
        src_ref=coef,
        dst_ref=coef_low,
        send_sem=coef_sem.at[0],
        recv_sem=coef_sem.at[1],
        device_id={"hel": lax.rem(hel + 1, hels)},
        device_id_type=MESH,
    )

    def hel_up(step, x, c):
        return pltpu.make_async_remote_copy(
            src_ref=x.at[block(c)],
            dst_ref=low.at[step, block(c)],
            send_sem=hel_send.at[step, 0, c],
            recv_sem=hel_recv.at[step, 0, c],
            device_id={"hel": lax.rem(hel + 1, hels)},
            device_id_type=MESH,
        )

    def hel_down(step, x, c):
        return pltpu.make_async_remote_copy(
            src_ref=x.at[block(c)],
            dst_ref=high.at[step, block(c)],
            send_sem=hel_send.at[step, 1, c],
            recv_sem=hel_recv.at[step, 1, c],
            device_id={"hel": lax.rem(hel - 1 + hels, hels)},
            device_id_type=MESH,
        )

    def hel_start(step, x, c):
        @pl.when(has_high)
        def _():
            hel_up(step, x, c).start()

        @pl.when(has_low)
        def _():
            hel_down(step, x, c).start()

    def hel_wait_recv(step, x, c):
        @pl.when(has_low)
        def _():
            hel_up(step, x, c).wait_recv()

        @pl.when(has_high)
        def _():
            hel_down(step, x, c).wait_recv()

    def hel_wait_send(step, x, c):
        @pl.when(has_high)
        def _():
            hel_up(step, x, c).wait_send()

        @pl.when(has_low)
        def _():
            hel_down(step, x, c).wait_send()

    def trailing(make, copy):
        @pl.loop(0, n - 1)
        def _(i):
            make(i)

            @pl.when(i > 0)
            def _():
                copy(i - 1).start()

    loads[0].wait()
    for l in range(width // 128):
        part = pot_in[:, :, 128 * l : 128 * (l + 1)].astype(jnp.float32)
        pot_wide[l] = part.reshape(pot_wide.shape[1:])

    def picked(ref, c, count):
        return jnp.concatenate(
            [ref[l, pl.ds(c, rows, stride=n), :] for l in range(count)], axis=1
        )

    def make_pot(i):
        send_pot[i] = picked(pot_wide, partner(i), width // 128).astype(jnp.bfloat16)

    trailing(make_pot, pot_copy)
    pot[hel, block(me)] = picked(pot_wide, me, width // 128).astype(jnp.bfloat16)
    pot_copy(n - 2).start()

    each_lane(newer_load, "wait")

    def make_new(i):
        mine1[block(partner(i))] = picked(newer_v, partner(i), ang // 128).astype(jnp.bfloat16)

    trailing(make_new, new_copy)
    mine1[block(me)] = picked(newer_v, me, ang // 128).astype(jnp.bfloat16)
    new_copy(n - 2).start()

    @pl.loop(0, n)
    def _(c):
        hel_start(0, mine1, c)

    x1[block(me)] = mine1[block(me)]
    loads[1].wait()
    loads[2].wait()

    @pl.loop(0, n - 1)
    def _(i):
        damp_copy(i).start()

    @pl.when(has_high)
    def _():
        coef_copy.start()

    damp_all[me] = damp_own[...]

    @pl.when(jnp.logical_not(has_low))
    def _():
        low[...] = jnp.zeros_like(low)
        coef_low[...] = jnp.zeros_like(coef_low)

    @pl.when(jnp.logical_not(has_high))
    def _():
        high[...] = jnp.zeros_like(high)

    line = lax.broadcasted_iota(jnp.int32, (rows, rows), 0)
    lane = lax.broadcasted_iota(jnp.int32, (rows, rows), 1)

    def column(row):
        diagonal = jnp.where(line == lane, jnp.broadcast_to(row, (rows, rows)), 0.0)
        return jnp.broadcast_to(jnp.sum(diagonal, axis=1, keepdims=True), (rows, 128))

    damp_col[block(me)] = column(damp_own[...])
    loads[3].wait()
    for c in range(n):
        part = weight_all[:, c * rows : (c + 1) * rows]
        weight_col[c * rows : (c + 1) * rows] = column(part)

    loads[4].wait()
    loads[5].wait()
    for l in range(ang // 128):
        part = pot_full[:, :, 128 * l : 128 * (l + 1)].astype(jnp.float32)
        pot_wide[l] = part.reshape(pot_wide.shape[1:])

    @pl.loop(0, n)
    def _(c):
        pot_mine[block(c)] = picked(pot_wide, c, ang // 128).astype(jnp.bfloat16)

    everything = pl.ds(0, n * rows)

    def from_grid(span):
        return lax.dot_general(
            grid[span], tr[...], (((1,), (1,)), ((), ())), preferred_element_type=jnp.float32
        )

    values = jnp.dot(mine1[...], tr[...], preferred_element_type=jnp.float32)
    grid[...] = (values * pot_mine[...].astype(jnp.float32)).astype(jnp.bfloat16)
    total[...] = from_grid(everything)

    @pl.loop(0, n - 1)
    def _(i):
        pot_copy(i).wait_recv()

    @pl.loop(1, hels)
    def _(j):
        pot_share(j).start()

    @pl.when(has_low)
    def _():
        coef_copy.wait_recv()

    lower_coef = coef_low[...].astype(jnp.float32)
    upper_coef = coef[...].astype(jnp.float32)

    def mixed(step, span):
        below = lower_coef * low[step, span].astype(jnp.float32)
        return below + upper_coef * high[step, span].astype(jnp.float32)

    each_lane(older_load, "wait")
    my_damp = damp_col[block(me), 0:1]
    my_weight = weight_col[block(me), 0:1]

    def make_old(c):
        hel_wait_recv(0, mine1, c)
        applied = SCALE_FACTOR * (total[block(c)] + my_weight * mixed(0, block(c)))
        prev = picked(older_v, c, ang // 128)
        mine0[block(c)] = (my_damp * (2.0 * applied - my_damp * prev)).astype(jnp.bfloat16)

    def send_old(i):
        make_old(partner(i))

    trailing(send_old, old_copy)
    old_copy(n - 2).start()
    make_old(me)
    x0[block(me)] = mine0[block(me)]

    @pl.loop(0, n - 1)
    def _(i):
        damp_copy(i).wait_recv()

    @pl.loop(0, n)
    def _(c):
        damp_col[block(c)] = column(damp_all[c])

    def near_side(visit):
        @pl.loop(0, half - 1)
        def _(m):
            visit(2 * m + 1)

    def far_side(first, last, visit):
        @pl.loop(first, last)
        def _(s):
            visit(across(s))

    loads[6].wait()

    @pl.loop(0, n - 1)
    def _(i):
        new_copy(i).wait_recv()

    total[...] = jnp.dot(kin[...], x1[...], preferred_element_type=jnp.float32)

    @pl.loop(1, hels)
    def _(j):
        pot_share(j).wait_recv()

    def to_grid(x, span):
        values = jnp.dot(x[span], tr[...], preferred_element_type=jnp.float32)
        for t in range(hels):
            part = values[:, t * width : (t + 1) * width] * pot[t, span].astype(jnp.float32)
            grid[span, t * width : (t + 1) * width] = part.astype(jnp.bfloat16)

    def multiply(x):
        to_grid(x, everything)
        radial = jnp.dot(kin[...], x[...], preferred_element_type=jnp.float32)
        total[...] = from_grid(everything) + radial

    def finish(step, whole, prev, c):
        span = block(c)
        damp = damp_col[span, 0:1]
        applied = SCALE_FACTOR * (whole + weight_col[span, 0:1] * mixed(step, span))
        following = damp * (2.0 * applied - damp * prev[span].astype(jnp.float32))
        return following.astype(jnp.bfloat16)

    def advance(c):
        span = block(c)
        scale = 2.0 * SCALE_FACTOR * damp_col[span, 0:1]
        x2[span] = (scale * total[span] + x0[span].astype(jnp.float32)).astype(jnp.bfloat16)
        hel_start(1, x2, c)

    def stretch(first, count):
        return pl.ds(pl.multiple_of(first * rows, count * rows), count * rows)

    ours = stretch(side * half, half)
    early = stretch((1 - side) * (half + near), far)
    late = stretch(half - side * near, near)

    def spread(to, source):
        return jnp.dot(kin[to, source], x2[source], preferred_element_type=jnp.float32)

    def turn(span):
        to_grid(x2, span)
        second[span] += from_grid(span)

    def old_arrived(i):
        old_copy(i).wait_recv()
        advance(partner(i))

    advance(me)
    near_side(old_arrived)
    second[...] = spread(everything, ours)
    turn(ours)
    far_side(near, half, old_arrived)
    second[...] += spread(everything, early)
    turn(early)
    far_side(0, near, old_arrived)

    def make3(c):
        hel_wait_recv(1, x2, c)
        x3[block(c)] = finish(1, second[block(c)], x1, c)

    def send3(i):
        make3(partner(i))
        out3_copy(i).start()
        hel_start(2, x3, partner(i))

    second[early] += spread(early, late)
    def alternate(first, last, visit):
        @pl.loop(first, last)
        def _(m):
            visit(across((m + near) % half))

            @pl.when(m < half - 1)
            def _():
                visit(2 * m + 1)

    second[ours] += spread(ours, late)
    alternate(0, far, send3)
    second[late] += spread(late, late)
    turn(late)
    alternate(far, half, send3)
    make3(me)
    hel_start(2, x3, me)

    multiply(x3)

    def make4(c):
        hel_wait_recv(2, x3, c)
        x4[block(c)] = finish(2, total[block(c)], x2, c)

    def send4(i):
        make4(partner(i))
        out4_copy(i).start()

    alternate(0, half, send4)
    make4(me)

    def interleave(res, piece, c):
        for l in range(ang // 128):
            res[l, pl.ds(c, rows, stride=n), :] = piece[:, l * 128 : (l + 1) * 128].astype(
                jnp.float32
            )

    interleave(res3, x3[block(me)], me)
    interleave(res4, x4[block(me)], me)

    def arrived3(i):
        out3_copy(i).wait_recv()
        interleave(res3, back3[partner(i)], partner(i))

    def arrived4(i):
        out4_copy(i).wait_recv()
        interleave(res4, back4[partner(i)], partner(i))

    for arrived in (arrived3, arrived4):
        near_side(arrived)
        far_side(near, half, arrived)
        far_side(0, near, arrived)

    @pl.loop(0, n - 1)
    def _(i):
        for copy in (pot_copy, new_copy, old_copy, damp_copy, out3_copy, out4_copy):
            copy(i).wait_send()

    @pl.loop(1, hels)
    def _(j):
        pot_share(j).wait_send()

    @pl.when(has_high)
    def _():
        coef_copy.wait_send()

    @pl.loop(0, n)
    def _(c):
        hel_wait_send(0, mine1, c)
        hel_wait_send(1, x2, c)
        hel_wait_send(2, x3, c)


def place_kernel(res3, res4, out_old, out_new, sem):
    copies = [
        pltpu.make_async_copy(
            res.at[l], out.at[:, pl.ds(128 * l, 128)], sem.at[s, l]
        )
        for s, (res, out) in enumerate(((res3, out_old), (res4, out_new)))
        for l in range(res.shape[0])
    ]
    for copy in copies:
        copy.start()
    for copy in copies:
        copy.wait()


def one_vibration(
    older_packet, newer_packet, kinetic, transform, potential, coupling, radial_weight, damping
):
    _, rows, n, ang = newer_packet.shape
    hels = lax.axis_size("hel")
    width = ang // hels
    points = n * rows
    bf16, f32 = jnp.bfloat16, jnp.float32
    vector = pltpu.VMEM((points, ang), bf16)
    blocks = pltpu.VMEM((n, rows, ang), bf16)
    wide = pltpu.VMEM((points, ang), f32)
    flat = jax.ShapeDtypeStruct((points, ang), f32)
    anywhere = pl.BlockSpec(memory_space=pl.ANY)
    inside = pl.BlockSpec(memory_space=pltpu.VMEM)
    sem = pltpu.SemaphoreType.DMA
    groups = ang // 128
    result = pltpu.VMEM((groups, points, 128), f32)
    results = pl.pallas_call(
        functools.partial(packet_kernel, n, hels),
        out_shape=(result, result),
        in_specs=[anywhere] * 8,
        out_specs=(inside, inside),
        scratch_shapes=[
            pltpu.VMEM((groups, points, 128), f32),
            pltpu.VMEM((groups, points, 128), f32),
            pltpu.VMEM((points, points), bf16),
            pltpu.VMEM((ang, ang), bf16),
            pltpu.VMEM((rows, n, width), bf16),
            pltpu.VMEM((rows, n, ang), bf16),
            pltpu.VMEM((groups, points, 128), f32),
            pltpu.VMEM((1, ang), bf16),
            pltpu.VMEM((1, ang), bf16),
            pltpu.VMEM((1, rows), f32),
            pltpu.VMEM((n, 1, rows), f32),
            pltpu.VMEM((1, points), f32),
            pltpu.VMEM((points, 128), f32),
            pltpu.VMEM((points, 128), f32),
            pltpu.VMEM((n, rows, width), bf16),
            vector,
            vector,
            vector,
            pltpu.VMEM((hels, points, width), bf16),
            vector,
            vector,
            vector,
            vector,
            vector,
            wide,
            wide,
            vector,
            pltpu.VMEM((STEPS, points, ang), bf16),
            pltpu.VMEM((STEPS, points, ang), bf16),
            blocks,
            blocks,
            sem((7,)),
            sem((2, groups)),
            sem((6, n)),
            sem((6, n)),
            sem((hels,)),
            sem((hels,)),
            sem((STEPS, 2, n)),
            sem((STEPS, 2, n)),
            sem((2,)),
        ],
        compiler_params=pltpu.CompilerParams(
            collective_id=0, has_side_effects=True, vmem_limit_bytes=VMEM_LIMIT
        ),
    )(
        newer_packet.reshape(points, ang),
        older_packet.reshape(points, ang),
        kinetic,
        transform[0],
        potential,
        coupling,
        radial_weight.reshape(1, points),
        damping.reshape(1, rows),
    )
    outs = pl.pallas_call(
        place_kernel,
        out_shape=(flat, flat),
        in_specs=[inside] * 2,
        out_specs=(anywhere, anywhere),
        scratch_shapes=[sem((2, groups))],
        compiler_params=pltpu.CompilerParams(vmem_limit_bytes=4 * 1024 * 1024),
    )(*results)
    shape = newer_packet.shape
    return outs[0].reshape(shape), outs[1].reshape(shape)


def fits(packet):
    hel_rows, rows, vibs, ang = packet.shape
    hels = lax.axis_size("hel")
    return (
        STEPS == 3
        and hel_rows == 1
        and vibs == lax.axis_size("rad")
        and vibs > 1
        and vibs & (vibs - 1) == 0
        and vibs >= 4
        and rows * vibs % 512 == 0
        and hels > 1
        and rows % 16 == 0
        and ang % (hels * 128) == 0
        and rows * vibs <= 512
        and ang <= 1024
    )


def whole_body(older_packet, newer_packet, *rest):
    if fits(newer_packet):
        return one_vibration(older_packet, newer_packet, *rest)
    if newer_packet.shape[2] % lax.axis_size("rad") == 0:
        return by_vibration(older_packet, newer_packet, *rest)
    return body(older_packet, newer_packet, *rest)


def solution(mesh):
    return jax.shard_map(
        whole_body,
        mesh=mesh,
        in_specs=(
            P("hel", "rad", None, None),
            P("hel", "rad", None, None),
            P(),
            P("hel", None, None),
            P("rad", None, None),
            P("hel", None),
            P(),
            P("rad"),
        ),
        out_specs=(P("hel", "rad", None, None), P("hel", "rad", None, None)),
        check_vma=False,
    )
```

```python
import functools

import jax
import jax.numpy as jnp
from jax import lax
from jax.experimental import pallas as pl
from jax.experimental.pallas import tpu as pltpu
from jax.sharding import PartitionSpec as P

STEPS = 3


SCALE_FACTOR = 0.35
VMEM_LIMIT = 60 * 1024 * 1024 - 128 * 1024


def from_behind(array, axis, by):
    devices = lax.axis_size(axis)
    pairs = [(i, i + by) for i in range(devices) if 0 <= i + by < devices]
    return lax.ppermute(array, axis, pairs)


def coriolis_term(block, coefs, weights):
    lower_block, lower_coefs = from_behind((block, coefs), "hel", 1)
    upper_block = from_behind(block, "hel", -1)
    below = jnp.concatenate([lower_block, block[:-1]], axis=0).astype(jnp.float32)
    below_coefs = jnp.concatenate([lower_coefs, coefs[:-1]], axis=0).astype(jnp.float32)
    above = jnp.concatenate([block[1:], upper_block], axis=0).astype(jnp.float32)
    mixed = below_coefs[:, None, :] * below + coefs.astype(jnp.float32)[:, None, :] * above
    return weights[None, :, None] * mixed


def body(
    older_packet, newer_packet, kinetic, transform, potential, coupling, radial_weight, damping
):
    hel_rows, rad_rows, vib_count, ang_count = newer_packet.shape
    flat_width = vib_count * ang_count
    rank = lax.axis_index("rad")
    previous = older_packet.reshape(hel_rows, rad_rows, flat_width)
    current = newer_packet.reshape(hel_rows, rad_rows, flat_width)
    potential_flat = potential.astype(jnp.float32).reshape(1, rad_rows * vib_count, ang_count)
    tiled_coefs = jnp.tile(coupling, (1, vib_count))
    damp = damping[None, :, None]
    for _ in range(STEPS):
        rounded = current.astype(jnp.bfloat16)
        regrouped = lax.all_to_all(rounded, "rad", split_axis=2, concat_axis=1, tiled=True)
        kinetic_term = jnp.einsum(
            "rs,ksc->krc", kinetic, regrouped, preferred_element_type=jnp.float32
        )
        returned = lax.all_to_all(kinetic_term, "rad", split_axis=1, concat_axis=2, tiled=True)
        start = rank * rad_rows
        local_weights = lax.dynamic_slice_in_dim(radial_weight, start, rad_rows, 0)
        summed = returned + coriolis_term(rounded, tiled_coefs, local_weights)
        off_grid = summed.astype(jnp.bfloat16).astype(jnp.float32)
        angular_rows = rounded.reshape(hel_rows, rad_rows * vib_count, ang_count)
        grid = jnp.einsum(
            "kna,kag->kng", angular_rows, transform, preferred_element_type=jnp.float32
        )
        grid_values = (grid * potential_flat).astype(jnp.bfloat16)
        angular_part = jnp.einsum(
            "kng,kag->kna", grid_values, transform, preferred_element_type=jnp.float32
        )
        applied = SCALE_FACTOR * (off_grid + angular_part.reshape(hel_rows, rad_rows, flat_width))
        following = damp * (2.0 * applied - damp * previous)
        previous = current
        current = following
    shape = (hel_rows, rad_rows, vib_count, ang_count)
    return (previous.reshape(shape), current.reshape(shape))


def by_vibration(
    older_packet, newer_packet, kinetic, transform, potential, coupling, radial_weight, damping
):
    hel_rows, rad_rows, vib_count, ang_count = newer_packet.shape
    devices = lax.axis_size("rad")

    def scatter(array):
        return lax.all_to_all(array, "rad", split_axis=2, concat_axis=1, tiled=True)

    rounded = scatter(newer_packet.astype(jnp.bfloat16))
    previous = scatter(older_packet.astype(jnp.bfloat16)).astype(jnp.float32)
    pot = scatter(potential[None])[0].astype(jnp.float32)
    damp = lax.all_gather(damping, "rad", tiled=True)[None, :, None, None]
    weight = radial_weight[None, :, None, None]
    current = rounded.astype(jnp.float32)
    lower_coefs = from_behind(coupling, "hel", 1)
    coefs = jnp.concatenate([lower_coefs, coupling], axis=0).astype(jnp.float32)
    coefs = coefs[:, None, None, :]
    history = []
    for step in range(STEPS):
        lower = from_behind(rounded[-1:], "hel", 1)
        upper = from_behind(rounded[:1], "hel", -1)
        padded = jnp.concatenate([lower, rounded, upper], axis=0).astype(jnp.float32)
        mixed = coefs[:-1] * padded[:-2] + coefs[1:] * padded[2:]
        radial = jnp.einsum(
            "rs,ksva->krva", kinetic, rounded, preferred_element_type=jnp.float32
        )
        off_grid = radial + weight * mixed
        grid = jnp.einsum(
            "krva,kag->krvg", rounded, transform, preferred_element_type=jnp.float32
        )
        grid_values = (grid * pot[None]).astype(jnp.bfloat16)
        angular = jnp.einsum(
            "krvg,kag->krva", grid_values, transform, preferred_element_type=jnp.float32
        )
        applied = SCALE_FACTOR * (off_grid + angular)
        following = damp * (2.0 * applied - damp * previous)
        previous = current
        current = following
        rounded = current.astype(jnp.bfloat16)
        history.append(rounded)

    def gather(array):
        back = lax.all_to_all(array, "rad", split_axis=1, concat_axis=2, tiled=True)
        return back.astype(jnp.float32)

    return gather(history[-2]), gather(history[-1])


MESH = pl.DeviceIdType.MESH
POT, NEW, OLD, DAMP, OUT3, OUT4 = range(6)


def xor(a, b, n):
    bit, total = 1, 0
    while bit < n:
        total = total + bit * ((a // bit + b // bit) % 2)
        bit *= 2
    return total


def packet_kernel(
    n, hels,
    newer, older, kinetic, transform, potential, coupling, weight, damping,
    res3, res4,
    newer_v, older_v, kin, tr, pot_in, pot_full, pot_wide, coef, coef_low, damp_own, damp_all,
    weight_all, damp_col, weight_col, send_pot, pot_mine, mine0, mine1, pot, x0, x1, x2, x3, x4,
    total, second, grid, low, high, back3, back4,
    in_sem, lane_sem, rad_send, rad_recv, pot_send, pot_recv, hel_send, hel_recv, coef_sem,
):
    me = lax.axis_index("rad")
    hel = lax.axis_index("hel")
    rows = send_pot.shape[1]
    ang = newer.shape[1]
    width = ang // hels
    half = n // 2
    far = half // 2
    near = half - far
    side = me // half
    has_low = hel > 0
    has_high = hel < hels - 1

    def partner(i):
        odd = i % 2
        return xor(me, odd * ((i + 1) // 2) + (1 - odd) * (half + i // 2), n)

    def across(s):
        s = xor(s, me % near, half)
        return 2 * xor(me % half, s + side * (half - 1 - 2 * s), half)

    def block(c):
        return pl.ds(pl.multiple_of(c * rows, rows), rows)

    barrier = pltpu.get_barrier_semaphore()

    @pl.loop(1, n)
    def _(j):
        pl.semaphore_signal(
            barrier, inc=1, device_id={"rad": lax.rem(me + j, n)}, device_id_type=MESH
        )

    @pl.loop(1, hels)
    def _(j):
        pl.semaphore_signal(
            barrier, inc=1, device_id={"hel": lax.rem(hel + j, hels)}, device_id_type=MESH
        )

    loads = [
        pltpu.make_async_copy(src, dst, in_sem.at[s])
        for s, (src, dst) in enumerate(
            (
                (potential.at[:, :, pl.ds(pl.multiple_of(hel * width, width), width)], pot_in),
                (damping, damp_own),
                (coupling, coef),
                (weight, weight_all),
                (transform, tr),
                (potential, pot_full),
                (kinetic, kin),
            )
        )
    ]

    def lanes(l):
        return pl.ds(pl.multiple_of(l * 128, 128), 128)

    def newer_load(l):
        return pltpu.make_async_copy(newer.at[:, lanes(l)], newer_v.at[l], lane_sem.at[0, l])

    def older_load(l):
        return pltpu.make_async_copy(older.at[:, lanes(l)], older_v.at[l], lane_sem.at[1, l])

    def each_lane(copy, method):
        @pl.loop(0, ang // 128)
        def _(l):
            getattr(copy(l), method)()

    for load in loads[:3]:
        load.start()
    each_lane(newer_load, "start")
    each_lane(older_load, "start")
    for load in loads[3:]:
        load.start()

    pl.semaphore_wait(barrier, n + hels - 2)

    def over_rad(kind, src, dst, i):
        return pltpu.make_async_remote_copy(
            src_ref=src,
            dst_ref=dst,
            send_sem=rad_send.at[kind, i],
            recv_sem=rad_recv.at[kind, i],
            device_id={"rad": partner(i)},
            device_id_type=MESH,
        )

    def pot_copy(i):
        return over_rad(POT, send_pot.at[i], pot.at[hel, block(me)], i)

    def new_copy(i):
        return over_rad(NEW, mine1.at[block(partner(i))], x1.at[block(me)], i)

    def old_copy(i):
        return over_rad(OLD, mine0.at[block(partner(i))], x0.at[block(me)], i)

    def damp_copy(i):
        return over_rad(DAMP, damp_own, damp_all.at[me], i)

    def out3_copy(i):
        return over_rad(OUT3, x3.at[block(partner(i))], back3.at[me], i)

    def out4_copy(i):
        return over_rad(OUT4, x4.at[block(partner(i))], back4.at[me], i)

    def pot_share(j):
        return pltpu.make_async_remote_copy(
            src_ref=pot.at[hel],
            dst_ref=pot.at[hel],
            send_sem=pot_send.at[j],
            recv_sem=pot_recv.at[j],
            device_id={"hel": lax.rem(hel + j, hels)},
            device_id_type=MESH,
        )

    coef_copy = pltpu.make_async_remote_copy(
        src_ref=coef,
        dst_ref=coef_low,
        send_sem=coef_sem.at[0],
        recv_sem=coef_sem.at[1],
        device_id={"hel": lax.rem(hel + 1, hels)},
        device_id_type=MESH,
    )

    def hel_up(step, x, c):
        return pltpu.make_async_remote_copy(
            src_ref=x.at[block(c)],
            dst_ref=low.at[step, block(c)],
            send_sem=hel_send.at[step, 0, c],
            recv_sem=hel_recv.at[step, 0, c],
            device_id={"hel": lax.rem(hel + 1, hels)},
            device_id_type=MESH,
        )

    def hel_down(step, x, c):
        return pltpu.make_async_remote_copy(
            src_ref=x.at[block(c)],
            dst_ref=high.at[step, block(c)],
            send_sem=hel_send.at[step, 1, c],
            recv_sem=hel_recv.at[step, 1, c],
            device_id={"hel": lax.rem(hel - 1 + hels, hels)},
            device_id_type=MESH,
        )

    def hel_start(step, x, c):
        @pl.when(has_high)
        def _():
            hel_up(step, x, c).start()

        @pl.when(has_low)
        def _():
            hel_down(step, x, c).start()

    def hel_wait_recv(step, x, c):
        @pl.when(has_low)
        def _():
            hel_up(step, x, c).wait_recv()

        @pl.when(has_high)
        def _():
            hel_down(step, x, c).wait_recv()

    def hel_wait_send(step, x, c):
        @pl.when(has_high)
        def _():
            hel_up(step, x, c).wait_send()

        @pl.when(has_low)
        def _():
            hel_down(step, x, c).wait_send()

    def trailing(make, copy):
        @pl.loop(0, n - 1)
        def _(i):
            make(i)

            @pl.when(i > 0)
            def _():
                copy(i - 1).start()

    loads[0].wait()
    for l in range(width // 128):
        part = pot_in[:, :, 128 * l : 128 * (l + 1)].astype(jnp.float32)
        pot_wide[l] = part.reshape(pot_wide.shape[1:])

    def picked(ref, c, count):
        return jnp.concatenate(
            [ref[l, pl.ds(c, rows, stride=n), :] for l in range(count)], axis=1
        )

    def make_pot(i):
        send_pot[i] = picked(pot_wide, partner(i), width // 128).astype(jnp.bfloat16)

    trailing(make_pot, pot_copy)
    pot[hel, block(me)] = picked(pot_wide, me, width // 128).astype(jnp.bfloat16)
    pot_copy(n - 2).start()

    each_lane(newer_load, "wait")

    def make_new(i):
        mine1[block(partner(i))] = picked(newer_v, partner(i), ang // 128).astype(jnp.bfloat16)

    trailing(make_new, new_copy)
    mine1[block(me)] = picked(newer_v, me, ang // 128).astype(jnp.bfloat16)
    new_copy(n - 2).start()

    @pl.loop(0, n)
    def _(c):
        hel_start(0, mine1, c)

    x1[block(me)] = mine1[block(me)]
    loads[1].wait()
    loads[2].wait()

    @pl.loop(0, n - 1)
    def _(i):
        damp_copy(i).start()

    @pl.when(has_high)
    def _():
        coef_copy.start()

    damp_all[me] = damp_own[...]

    @pl.when(jnp.logical_not(has_low))
    def _():
        low[...] = jnp.zeros_like(low)
        coef_low[...] = jnp.zeros_like(coef_low)

    @pl.when(jnp.logical_not(has_high))
    def _():
        high[...] = jnp.zeros_like(high)

    line = lax.broadcasted_iota(jnp.int32, (rows, rows), 0)
    lane = lax.broadcasted_iota(jnp.int32, (rows, rows), 1)

    def column(row):
        diagonal = jnp.where(line == lane, jnp.broadcast_to(row, (rows, rows)), 0.0)
        return jnp.broadcast_to(jnp.sum(diagonal, axis=1, keepdims=True), (rows, 128))

    damp_col[block(me)] = column(damp_own[...])
    loads[3].wait()
    for c in range(n):
        part = weight_all[:, c * rows : (c + 1) * rows]
        weight_col[c * rows : (c + 1) * rows] = column(part)

    loads[4].wait()
    loads[5].wait()
    for l in range(ang // 128):
        part = pot_full[:, :, 128 * l : 128 * (l + 1)].astype(jnp.float32)
        pot_wide[l] = part.reshape(pot_wide.shape[1:])

    @pl.loop(0, n)
    def _(c):
        pot_mine[block(c)] = picked(pot_wide, c, ang // 128).astype(jnp.bfloat16)

    everything = pl.ds(0, n * rows)

    def from_grid(span):
        return lax.dot_general(
            grid[span], tr[...], (((1,), (1,)), ((), ())), preferred_element_type=jnp.float32
        )

    values = jnp.dot(mine1[...], tr[...], preferred_element_type=jnp.float32)
    grid[...] = (values * pot_mine[...].astype(jnp.float32)).astype(jnp.bfloat16)
    total[...] = from_grid(everything)

    @pl.loop(0, n - 1)
    def _(i):
        pot_copy(i).wait_recv()

    @pl.loop(1, hels)
    def _(j):
        pot_share(j).start()

    @pl.when(has_low)
    def _():
        coef_copy.wait_recv()

    lower_coef = coef_low[...].astype(jnp.float32)
    upper_coef = coef[...].astype(jnp.float32)

    def mixed(step, span):
        below = lower_coef * low[step, span].astype(jnp.float32)
        return below + upper_coef * high[step, span].astype(jnp.float32)

    each_lane(older_load, "wait")
    my_damp = damp_col[block(me), 0:1]
    my_weight = weight_col[block(me), 0:1]

    def make_old(c):
        hel_wait_recv(0, mine1, c)
        applied = SCALE_FACTOR * (total[block(c)] + my_weight * mixed(0, block(c)))
        prev = picked(older_v, c, ang // 128)
        mine0[block(c)] = (my_damp * (2.0 * applied - my_damp * prev)).astype(jnp.bfloat16)

    def send_old(i):
        make_old(partner(i))

    trailing(send_old, old_copy)
    old_copy(n - 2).start()
    make_old(me)
    x0[block(me)] = mine0[block(me)]

    @pl.loop(0, n - 1)
    def _(i):
        damp_copy(i).wait_recv()

    @pl.loop(0, n)
    def _(c):
        damp_col[block(c)] = column(damp_all[c])

    def near_side(visit):
        @pl.loop(0, half - 1)
        def _(m):
            visit(2 * m + 1)

    def far_side(first, last, visit):
        @pl.loop(first, last)
        def _(s):
            visit(across(s))

    loads[6].wait()

    @pl.loop(0, n - 1)
    def _(i):
        new_copy(i).wait_recv()

    total[...] = jnp.dot(kin[...], x1[...], preferred_element_type=jnp.float32)

    @pl.loop(1, hels)
    def _(j):
        pot_share(j).wait_recv()

    def to_grid(x, span):
        values = jnp.dot(x[span], tr[...], preferred_element_type=jnp.float32)
        for t in range(hels):
            part = values[:, t * width : (t + 1) * width] * pot[t, span].astype(jnp.float32)
            grid[span, t * width : (t + 1) * width] = part.astype(jnp.bfloat16)

    def multiply(x):
        to_grid(x, everything)
        radial = jnp.dot(kin[...], x[...], preferred_element_type=jnp.float32)
        total[...] = from_grid(everything) + radial

    def finish(step, whole, prev, c):
        span = block(c)
        damp = damp_col[span, 0:1]
        applied = SCALE_FACTOR * (whole + weight_col[span, 0:1] * mixed(step, span))
        following = damp * (2.0 * applied - damp * prev[span].astype(jnp.float32))
        return following.astype(jnp.bfloat16)

    def advance(c):
        span = block(c)
        scale = 2.0 * SCALE_FACTOR * damp_col[span, 0:1]
        x2[span] = (scale * total[span] + x0[span].astype(jnp.float32)).astype(jnp.bfloat16)
        hel_start(1, x2, c)

    def stretch(first, count):
        return pl.ds(pl.multiple_of(first * rows, count * rows), count * rows)

    ours = stretch(side * half, half)
    early = stretch((1 - side) * (half + near), far)
    late = stretch(half - side * near, near)

    def spread(to, source):
        return jnp.dot(kin[to, source], x2[source], preferred_element_type=jnp.float32)

    def turn(span):
        to_grid(x2, span)
        second[span] += from_grid(span)

    def old_arrived(i):
        old_copy(i).wait_recv()
        advance(partner(i))

    advance(me)
    near_side(old_arrived)
    second[...] = spread(everything, ours)
    turn(ours)
    far_side(near, half, old_arrived)
    second[...] += spread(everything, early)
    turn(early)
    far_side(0, near, old_arrived)

    def make3(c):
        hel_wait_recv(1, x2, c)
        x3[block(c)] = finish(1, second[block(c)], x1, c)

    def send3(i):
        make3(partner(i))
        out3_copy(i).start()
        hel_start(2, x3, partner(i))

    second[early] += spread(early, late)
    far_side(near, half, send3)
    second[ours] += spread(ours, late)
    send3(1)
    second[late] += spread(late, late)
    turn(late)

    @pl.loop(0, near)
    def _(s):
        send3(across(s))

        @pl.when(s + 2 < half)
        def _():
            send3(2 * s + 3)

    @pl.loop(near + 1, half - 1)
    def _(m):
        send3(2 * m + 1)

    make3(me)
    hel_start(2, x3, me)

    multiply(x3)

    def make4(c):
        hel_wait_recv(2, x3, c)
        x4[block(c)] = finish(2, total[block(c)], x2, c)

    def fill4(i):
        make4(partner(i))

    pl.loop(0, n - 1)(fill4)

    def start4(i):
        out4_copy(i).start()

    inner = jnp.logical_and(me >= half - near, me < half + near)

    @pl.when(inner)
    def _():
        @pl.loop(0, half)
        def _(m):
            start4(across((m + near) % half))

            @pl.when(m < half - 1)
            def _():
                start4(2 * m + 1)

    @pl.when(jnp.logical_not(inner))
    def _():
        near_side(start4)
        far_side(near, half, start4)
        far_side(0, near, start4)

    make4(me)

    def interleave(res, piece, c):
        for l in range(ang // 128):
            res[l, pl.ds(c, rows, stride=n), :] = piece[:, l * 128 : (l + 1) * 128].astype(
                jnp.float32
            )

    interleave(res3, x3[block(me)], me)
    interleave(res4, x4[block(me)], me)

    def arrived3(i):
        out3_copy(i).wait_recv()
        interleave(res3, back3[partner(i)], partner(i))

    def arrived4(i):
        out4_copy(i).wait_recv()
        interleave(res4, back4[partner(i)], partner(i))

    def arrivals(visit):
        near_side(visit)
        far_side(near, half, visit)
        far_side(0, near, visit)

    arrivals(arrived3)

    @pl.loop(0, n - 1)
    def _(i):
        for copy in (pot_copy, new_copy, old_copy, damp_copy, out3_copy):
            copy(i).wait_send()

    @pl.loop(1, hels)
    def _(j):
        pot_share(j).wait_send()

    @pl.when(has_high)
    def _():
        coef_copy.wait_send()

    @pl.loop(0, n)
    def _(c):
        hel_wait_send(0, mine1, c)
        hel_wait_send(1, x2, c)
        hel_wait_send(2, x3, c)

    arrivals(arrived4)

    @pl.loop(0, n - 1)
    def _(i):
        out4_copy(i).wait_send()


def place_kernel(res3, res4, out_old, out_new, sem):
    copies = [
        pltpu.make_async_copy(
            res.at[l], out.at[:, pl.ds(128 * l, 128)], sem.at[s, l]
        )
        for s, (res, out) in enumerate(((res3, out_old), (res4, out_new)))
        for l in range(res.shape[0])
    ]
    for copy in copies:
        copy.start()
    for copy in copies:
        copy.wait()


def one_vibration(
    older_packet, newer_packet, kinetic, transform, potential, coupling, radial_weight, damping
):
    _, rows, n, ang = newer_packet.shape
    hels = lax.axis_size("hel")
    width = ang // hels
    points = n * rows
    bf16, f32 = jnp.bfloat16, jnp.float32
    vector = pltpu.VMEM((points, ang), bf16)
    blocks = pltpu.VMEM((n, rows, ang), bf16)
    wide = pltpu.VMEM((points, ang), f32)
    flat = jax.ShapeDtypeStruct((points, ang), f32)
    anywhere = pl.BlockSpec(memory_space=pl.ANY)
    inside = pl.BlockSpec(memory_space=pltpu.VMEM)
    sem = pltpu.SemaphoreType.DMA
    groups = ang // 128
    result = pltpu.VMEM((groups, points, 128), f32)
    results = pl.pallas_call(
        functools.partial(packet_kernel, n, hels),
        out_shape=(result, result),
        in_specs=[anywhere] * 8,
        out_specs=(inside, inside),
        scratch_shapes=[
            pltpu.VMEM((groups, points, 128), f32),
            pltpu.VMEM((groups, points, 128), f32),
            pltpu.VMEM((points, points), bf16),
            pltpu.VMEM((ang, ang), bf16),
            pltpu.VMEM((rows, n, width), bf16),
            pltpu.VMEM((rows, n, ang), bf16),
            pltpu.VMEM((groups, points, 128), f32),
            pltpu.VMEM((1, ang), bf16),
            pltpu.VMEM((1, ang), bf16),
            pltpu.VMEM((1, rows), f32),
            pltpu.VMEM((n, 1, rows), f32),
            pltpu.VMEM((1, points), f32),
            pltpu.VMEM((points, 128), f32),
            pltpu.VMEM((points, 128), f32),
            pltpu.VMEM((n, rows, width), bf16),
            vector,
            vector,
            vector,
            pltpu.VMEM((hels, points, width), bf16),
            vector,
            vector,
            vector,
            vector,
            vector,
            wide,
            wide,
            vector,
            pltpu.VMEM((STEPS, points, ang), bf16),
            pltpu.VMEM((STEPS, points, ang), bf16),
            blocks,
            blocks,
            sem((7,)),
            sem((2, groups)),
            sem((6, n)),
            sem((6, n)),
            sem((hels,)),
            sem((hels,)),
            sem((STEPS, 2, n)),
            sem((STEPS, 2, n)),
            sem((2,)),
        ],
        compiler_params=pltpu.CompilerParams(
            collective_id=0, has_side_effects=True, vmem_limit_bytes=VMEM_LIMIT
        ),
    )(
        newer_packet.reshape(points, ang),
        older_packet.reshape(points, ang),
        kinetic,
        transform[0],
        potential,
        coupling,
        radial_weight.reshape(1, points),
        damping.reshape(1, rows),
    )
    outs = pl.pallas_call(
        place_kernel,
        out_shape=(flat, flat),
        in_specs=[inside] * 2,
        out_specs=(anywhere, anywhere),
        scratch_shapes=[sem((2, groups))],
        compiler_params=pltpu.CompilerParams(vmem_limit_bytes=4 * 1024 * 1024),
    )(*results)
    shape = newer_packet.shape
    return outs[0].reshape(shape), outs[1].reshape(shape)


def fits(packet):
    hel_rows, rows, vibs, ang = packet.shape
    hels = lax.axis_size("hel")
    return (
        STEPS == 3
        and hel_rows == 1
        and vibs == lax.axis_size("rad")
        and vibs > 1
        and vibs & (vibs - 1) == 0
        and vibs >= 4
        and rows * vibs % 512 == 0
        and hels > 1
        and rows % 16 == 0
        and ang % (hels * 128) == 0
        and rows * vibs <= 512
        and ang <= 1024
    )


def whole_body(older_packet, newer_packet, *rest):
    if fits(newer_packet):
        return one_vibration(older_packet, newer_packet, *rest)
    if newer_packet.shape[2] % lax.axis_size("rad") == 0:
        return by_vibration(older_packet, newer_packet, *rest)
    return body(older_packet, newer_packet, *rest)


def solution(mesh):
    return jax.shard_map(
        whole_body,
        mesh=mesh,
        in_specs=(
            P("hel", "rad", None, None),
            P("hel", "rad", None, None),
            P(),
            P("hel", None, None),
            P("rad", None, None),
            P("hel", None),
            P(),
            P("rad"),
        ),
        out_specs=(P("hel", "rad", None, None), P("hel", "rad", None, None)),
        check_vma=False,
    )
```

```python
import functools

import jax
import jax.numpy as jnp
from jax import lax
from jax.experimental import pallas as pl
from jax.experimental.pallas import tpu as pltpu
from jax.sharding import PartitionSpec as P

STEPS = 3


SCALE_FACTOR = 0.35
VMEM_LIMIT = 60 * 1024 * 1024 - 128 * 1024


def from_behind(array, axis, by):
    devices = lax.axis_size(axis)
    pairs = [(i, i + by) for i in range(devices) if 0 <= i + by < devices]
    return lax.ppermute(array, axis, pairs)


def coriolis_term(block, coefs, weights):
    lower_block, lower_coefs = from_behind((block, coefs), "hel", 1)
    upper_block = from_behind(block, "hel", -1)
    below = jnp.concatenate([lower_block, block[:-1]], axis=0).astype(jnp.float32)
    below_coefs = jnp.concatenate([lower_coefs, coefs[:-1]], axis=0).astype(jnp.float32)
    above = jnp.concatenate([block[1:], upper_block], axis=0).astype(jnp.float32)
    mixed = below_coefs[:, None, :] * below + coefs.astype(jnp.float32)[:, None, :] * above
    return weights[None, :, None] * mixed


def body(
    older_packet, newer_packet, kinetic, transform, potential, coupling, radial_weight, damping
):
    hel_rows, rad_rows, vib_count, ang_count = newer_packet.shape
    flat_width = vib_count * ang_count
    rank = lax.axis_index("rad")
    previous = older_packet.reshape(hel_rows, rad_rows, flat_width)
    current = newer_packet.reshape(hel_rows, rad_rows, flat_width)
    potential_flat = potential.astype(jnp.float32).reshape(1, rad_rows * vib_count, ang_count)
    tiled_coefs = jnp.tile(coupling, (1, vib_count))
    damp = damping[None, :, None]
    for _ in range(STEPS):
        rounded = current.astype(jnp.bfloat16)
        regrouped = lax.all_to_all(rounded, "rad", split_axis=2, concat_axis=1, tiled=True)
        kinetic_term = jnp.einsum(
            "rs,ksc->krc", kinetic, regrouped, preferred_element_type=jnp.float32
        )
        returned = lax.all_to_all(kinetic_term, "rad", split_axis=1, concat_axis=2, tiled=True)
        start = rank * rad_rows
        local_weights = lax.dynamic_slice_in_dim(radial_weight, start, rad_rows, 0)
        summed = returned + coriolis_term(rounded, tiled_coefs, local_weights)
        off_grid = summed.astype(jnp.bfloat16).astype(jnp.float32)
        angular_rows = rounded.reshape(hel_rows, rad_rows * vib_count, ang_count)
        grid = jnp.einsum(
            "kna,kag->kng", angular_rows, transform, preferred_element_type=jnp.float32
        )
        grid_values = (grid * potential_flat).astype(jnp.bfloat16)
        angular_part = jnp.einsum(
            "kng,kag->kna", grid_values, transform, preferred_element_type=jnp.float32
        )
        applied = SCALE_FACTOR * (off_grid + angular_part.reshape(hel_rows, rad_rows, flat_width))
        following = damp * (2.0 * applied - damp * previous)
        previous = current
        current = following
    shape = (hel_rows, rad_rows, vib_count, ang_count)
    return (previous.reshape(shape), current.reshape(shape))


def by_vibration(
    older_packet, newer_packet, kinetic, transform, potential, coupling, radial_weight, damping
):
    hel_rows, rad_rows, vib_count, ang_count = newer_packet.shape
    devices = lax.axis_size("rad")

    def scatter(array):
        return lax.all_to_all(array, "rad", split_axis=2, concat_axis=1, tiled=True)

    rounded = scatter(newer_packet.astype(jnp.bfloat16))
    previous = scatter(older_packet.astype(jnp.bfloat16)).astype(jnp.float32)
    pot = scatter(potential[None])[0].astype(jnp.float32)
    damp = lax.all_gather(damping, "rad", tiled=True)[None, :, None, None]
    weight = radial_weight[None, :, None, None]
    current = rounded.astype(jnp.float32)
    lower_coefs = from_behind(coupling, "hel", 1)
    coefs = jnp.concatenate([lower_coefs, coupling], axis=0).astype(jnp.float32)
    coefs = coefs[:, None, None, :]
    history = []
    for step in range(STEPS):
        lower = from_behind(rounded[-1:], "hel", 1)
        upper = from_behind(rounded[:1], "hel", -1)
        padded = jnp.concatenate([lower, rounded, upper], axis=0).astype(jnp.float32)
        mixed = coefs[:-1] * padded[:-2] + coefs[1:] * padded[2:]
        radial = jnp.einsum(
            "rs,ksva->krva", kinetic, rounded, preferred_element_type=jnp.float32
        )
        off_grid = radial + weight * mixed
        grid = jnp.einsum(
            "krva,kag->krvg", rounded, transform, preferred_element_type=jnp.float32
        )
        grid_values = (grid * pot[None]).astype(jnp.bfloat16)
        angular = jnp.einsum(
            "krvg,kag->krva", grid_values, transform, preferred_element_type=jnp.float32
        )
        applied = SCALE_FACTOR * (off_grid + angular)
        following = damp * (2.0 * applied - damp * previous)
        previous = current
        current = following
        rounded = current.astype(jnp.bfloat16)
        history.append(rounded)

    def gather(array):
        back = lax.all_to_all(array, "rad", split_axis=1, concat_axis=2, tiled=True)
        return back.astype(jnp.float32)

    return gather(history[-2]), gather(history[-1])


MESH = pl.DeviceIdType.MESH
POT, NEW, OLD, DAMP, OUT3, OUT4 = range(6)


def xor(a, b, n):
    bit, total = 1, 0
    while bit < n:
        total = total + bit * ((a // bit + b // bit) % 2)
        bit *= 2
    return total


def packet_kernel(
    n, hels,
    newer, older, kinetic, transform, potential, coupling, weight, damping,
    res3, res4,
    newer_v, older_v, kin, tr, pot_in, pot_full, pot_wide, coef, coef_low, damp_own, damp_all,
    weight_all, damp_col, weight_col, send_pot, pot_mine, mine0, mine1, pot, x0, x1, x2, x3, x4,
    total, second, grid, low, high, back3, back4,
    in_sem, lane_sem, rad_send, rad_recv, pot_send, pot_recv, hel_send, hel_recv, coef_sem,
):
    me = lax.axis_index("rad")
    hel = lax.axis_index("hel")
    rows = send_pot.shape[1]
    ang = newer.shape[1]
    width = ang // hels
    half = n // 2
    far = half // 2
    near = half - far
    side = me // half
    has_low = hel > 0
    has_high = hel < hels - 1

    def partner(i):
        odd = i % 2
        return xor(me, odd * ((i + 1) // 2) + (1 - odd) * (half + i // 2), n)

    def across(s):
        s = xor(s, me % near, half)
        return 2 * xor(me % half, s + side * (half - 1 - 2 * s), half)

    def block(c):
        return pl.ds(pl.multiple_of(c * rows, rows), rows)

    barrier = pltpu.get_barrier_semaphore()

    @pl.loop(1, n)
    def _(j):
        pl.semaphore_signal(
            barrier, inc=1, device_id={"rad": lax.rem(me + j, n)}, device_id_type=MESH
        )

    @pl.loop(1, hels)
    def _(j):
        pl.semaphore_signal(
            barrier, inc=1, device_id={"hel": lax.rem(hel + j, hels)}, device_id_type=MESH
        )

    loads = [
        pltpu.make_async_copy(src, dst, in_sem.at[s])
        for s, (src, dst) in enumerate(
            (
                (potential.at[:, :, pl.ds(pl.multiple_of(hel * width, width), width)], pot_in),
                (damping, damp_own),
                (coupling, coef),
                (weight, weight_all),
                (transform, tr),
                (potential, pot_full),
                (kinetic, kin),
            )
        )
    ]

    def lanes(l):
        return pl.ds(pl.multiple_of(l * 128, 128), 128)

    def newer_load(l):
        return pltpu.make_async_copy(newer.at[:, lanes(l)], newer_v.at[l], lane_sem.at[0, l])

    def older_load(l):
        return pltpu.make_async_copy(older.at[:, lanes(l)], older_v.at[l], lane_sem.at[1, l])

    def each_lane(copy, method):
        @pl.loop(0, ang // 128)
        def _(l):
            getattr(copy(l), method)()

    for load in loads[:3]:
        load.start()
    each_lane(newer_load, "start")
    each_lane(older_load, "start")
    for load in loads[3:]:
        load.start()

    pl.semaphore_wait(barrier, n + hels - 2)

    def over_rad(kind, src, dst, i):
        return pltpu.make_async_remote_copy(
            src_ref=src,
            dst_ref=dst,
            send_sem=rad_send.at[kind, i],
            recv_sem=rad_recv.at[kind, i],
            device_id={"rad": partner(i)},
            device_id_type=MESH,
        )

    def pot_copy(i):
        return over_rad(POT, send_pot.at[i], pot.at[hel, block(me)], i)

    def new_copy(i):
        return over_rad(NEW, mine1.at[block(partner(i))], x1.at[block(me)], i)

    def old_copy(i):
        return over_rad(OLD, mine0.at[block(partner(i))], x0.at[block(me)], i)

    def damp_copy(i):
        return over_rad(DAMP, damp_own, damp_all.at[me], i)

    def out3_copy(i):
        return over_rad(OUT3, x3.at[block(partner(i))], back3.at[me], i)

    def out4_copy(i):
        return over_rad(OUT4, x4.at[block(partner(i))], back4.at[me], i)

    def pot_share(j):
        return pltpu.make_async_remote_copy(
            src_ref=pot.at[hel],
            dst_ref=pot.at[hel],
            send_sem=pot_send.at[j],
            recv_sem=pot_recv.at[j],
            device_id={"hel": lax.rem(hel + j, hels)},
            device_id_type=MESH,
        )

    coef_copy = pltpu.make_async_remote_copy(
        src_ref=coef,
        dst_ref=coef_low,
        send_sem=coef_sem.at[0],
        recv_sem=coef_sem.at[1],
        device_id={"hel": lax.rem(hel + 1, hels)},
        device_id_type=MESH,
    )

    def hel_up(step, x, c):
        return pltpu.make_async_remote_copy(
            src_ref=x.at[block(c)],
            dst_ref=low.at[step, block(c)],
            send_sem=hel_send.at[step, 0, c],
            recv_sem=hel_recv.at[step, 0, c],
            device_id={"hel": lax.rem(hel + 1, hels)},
            device_id_type=MESH,
        )

    def hel_down(step, x, c):
        return pltpu.make_async_remote_copy(
            src_ref=x.at[block(c)],
            dst_ref=high.at[step, block(c)],
            send_sem=hel_send.at[step, 1, c],
            recv_sem=hel_recv.at[step, 1, c],
            device_id={"hel": lax.rem(hel - 1 + hels, hels)},
            device_id_type=MESH,
        )

    def hel_start(step, x, c):
        @pl.when(has_high)
        def _():
            hel_up(step, x, c).start()

        @pl.when(has_low)
        def _():
            hel_down(step, x, c).start()

    def hel_wait_recv(step, x, c):
        @pl.when(has_low)
        def _():
            hel_up(step, x, c).wait_recv()

        @pl.when(has_high)
        def _():
            hel_down(step, x, c).wait_recv()

    def hel_wait_send(step, x, c):
        @pl.when(has_high)
        def _():
            hel_up(step, x, c).wait_send()

        @pl.when(has_low)
        def _():
            hel_down(step, x, c).wait_send()

    def trailing(make, copy):
        @pl.loop(0, n - 1)
        def _(i):
            make(i)

            @pl.when(i > 0)
            def _():
                copy(i - 1).start()

    loads[0].wait()
    for l in range(width // 128):
        part = pot_in[:, :, 128 * l : 128 * (l + 1)].astype(jnp.float32)
        pot_wide[l] = part.reshape(pot_wide.shape[1:])

    def picked(ref, c, count):
        return jnp.concatenate(
            [ref[l, pl.ds(c, rows, stride=n), :] for l in range(count)], axis=1
        )

    def make_pot(i):
        send_pot[i] = picked(pot_wide, partner(i), width // 128).astype(jnp.bfloat16)

    trailing(make_pot, pot_copy)
    pot[hel, block(me)] = picked(pot_wide, me, width // 128).astype(jnp.bfloat16)
    pot_copy(n - 2).start()

    each_lane(newer_load, "wait")

    def make_new(i):
        mine1[block(partner(i))] = picked(newer_v, partner(i), ang // 128).astype(jnp.bfloat16)

    trailing(make_new, new_copy)
    mine1[block(me)] = picked(newer_v, me, ang // 128).astype(jnp.bfloat16)
    new_copy(n - 2).start()

    @pl.loop(0, n)
    def _(c):
        hel_start(0, mine1, c)

    x1[block(me)] = mine1[block(me)]
    loads[1].wait()
    loads[2].wait()

    @pl.loop(0, n - 1)
    def _(i):
        damp_copy(i).start()

    @pl.when(has_high)
    def _():
        coef_copy.start()

    damp_all[me] = damp_own[...]

    @pl.when(jnp.logical_not(has_low))
    def _():
        low[...] = jnp.zeros_like(low)
        coef_low[...] = jnp.zeros_like(coef_low)

    @pl.when(jnp.logical_not(has_high))
    def _():
        high[...] = jnp.zeros_like(high)

    line = lax.broadcasted_iota(jnp.int32, (rows, rows), 0)
    lane = lax.broadcasted_iota(jnp.int32, (rows, rows), 1)

    def column(row):
        diagonal = jnp.where(line == lane, jnp.broadcast_to(row, (rows, rows)), 0.0)
        return jnp.broadcast_to(jnp.sum(diagonal, axis=1, keepdims=True), (rows, 128))

    damp_col[block(me)] = column(damp_own[...])
    loads[3].wait()
    for c in range(n):
        part = weight_all[:, c * rows : (c + 1) * rows]
        weight_col[c * rows : (c + 1) * rows] = column(part)

    loads[4].wait()
    loads[5].wait()
    for l in range(ang // 128):
        part = pot_full[:, :, 128 * l : 128 * (l + 1)].astype(jnp.float32)
        pot_wide[l] = part.reshape(pot_wide.shape[1:])

    @pl.loop(0, n)
    def _(c):
        pot_mine[block(c)] = picked(pot_wide, c, ang // 128).astype(jnp.bfloat16)

    everything = pl.ds(0, n * rows)

    def from_grid(span):
        return lax.dot_general(
            grid[span], tr[...], (((1,), (1,)), ((), ())), preferred_element_type=jnp.float32
        )

    values = jnp.dot(mine1[...], tr[...], preferred_element_type=jnp.float32)
    grid[...] = (values * pot_mine[...].astype(jnp.float32)).astype(jnp.bfloat16)
    total[...] = from_grid(everything)

    @pl.loop(0, n - 1)
    def _(i):
        pot_copy(i).wait_recv()

    @pl.loop(1, hels)
    def _(j):
        pot_share(j).start()

    @pl.when(has_low)
    def _():
        coef_copy.wait_recv()

    lower_coef = coef_low[...].astype(jnp.float32)
    upper_coef = coef[...].astype(jnp.float32)

    def mixed(step, span):
        below = lower_coef * low[step, span].astype(jnp.float32)
        return below + upper_coef * high[step, span].astype(jnp.float32)

    each_lane(older_load, "wait")
    my_damp = damp_col[block(me), 0:1]
    my_weight = weight_col[block(me), 0:1]

    def make_old(c):
        hel_wait_recv(0, mine1, c)
        applied = SCALE_FACTOR * (total[block(c)] + my_weight * mixed(0, block(c)))
        prev = picked(older_v, c, ang // 128)
        mine0[block(c)] = (my_damp * (2.0 * applied - my_damp * prev)).astype(jnp.bfloat16)

    def send_old(i):
        make_old(partner(i))
        old_copy(i).start()

    @pl.loop(0, half)
    def _(s):
        send_old(across(s))

        @pl.when(s < half - 1)
        def _():
            send_old(2 * s + 1)

    make_old(me)
    x0[block(me)] = mine0[block(me)]

    @pl.loop(0, n - 1)
    def _(i):
        damp_copy(i).wait_recv()

    @pl.loop(0, n)
    def _(c):
        damp_col[block(c)] = column(damp_all[c])

    def near_side(visit):
        @pl.loop(0, half - 1)
        def _(m):
            visit(2 * m + 1)

    def far_side(first, last, visit):
        @pl.loop(first, last)
        def _(s):
            visit(across(s))

    loads[6].wait()

    @pl.loop(0, n - 1)
    def _(i):
        new_copy(i).wait_recv()

    total[...] = jnp.dot(kin[...], x1[...], preferred_element_type=jnp.float32)

    @pl.loop(1, hels)
    def _(j):
        pot_share(j).wait_recv()

    def to_grid(x, span):
        values = jnp.dot(x[span], tr[...], preferred_element_type=jnp.float32)
        for t in range(hels):
            part = values[:, t * width : (t + 1) * width] * pot[t, span].astype(jnp.float32)
            grid[span, t * width : (t + 1) * width] = part.astype(jnp.bfloat16)

    def multiply(x):
        to_grid(x, everything)
        radial = jnp.dot(kin[...], x[...], preferred_element_type=jnp.float32)
        total[...] = from_grid(everything) + radial

    def finish(step, whole, prev, c):
        span = block(c)
        damp = damp_col[span, 0:1]
        applied = SCALE_FACTOR * (whole + weight_col[span, 0:1] * mixed(step, span))
        following = damp * (2.0 * applied - damp * prev[span].astype(jnp.float32))
        return following.astype(jnp.bfloat16)

    def advance(c):
        span = block(c)
        scale = 2.0 * SCALE_FACTOR * damp_col[span, 0:1]
        x2[span] = (scale * total[span] + x0[span].astype(jnp.float32)).astype(jnp.bfloat16)
        hel_start(1, x2, c)

    def stretch(first, count):
        return pl.ds(pl.multiple_of(first * rows, count * rows), count * rows)

    ours = stretch(side * half, half)
    early = stretch((1 - side) * (half + near), far)
    late = stretch(half - side * near, near)

    def spread(to, source):
        return jnp.dot(kin[to, source], x2[source], preferred_element_type=jnp.float32)

    def turn(span):
        to_grid(x2, span)
        second[span] += from_grid(span)

    def old_arrived(i):
        old_copy(i).wait_recv()
        advance(partner(i))

    advance(me)
    near_side(old_arrived)
    second[...] = spread(everything, ours)
    turn(ours)
    far_side(near, half, old_arrived)
    second[...] += spread(everything, early)
    turn(early)
    far_side(0, near, old_arrived)

    def make3(c):
        hel_wait_recv(1, x2, c)
        x3[block(c)] = finish(1, second[block(c)], x1, c)

    def send3(i):
        make3(partner(i))
        out3_copy(i).start()

    second[early] += spread(early, late)
    far_side(near, half, send3)
    second[ours] += spread(ours, late)
    send3(1)
    second[late] += spread(late, late)
    turn(late)

    @pl.loop(0, near)
    def _(s):
        send3(across(s))

        @pl.when(s + 2 < half)
        def _():
            send3(2 * s + 3)

    @pl.loop(near + 1, half - 1)
    def _(m):
        send3(2 * m + 1)

    make3(me)

    @pl.loop(0, n)
    def _(c):
        hel_start(2, x3, c)

    multiply(x3)

    def make4(c):
        hel_wait_recv(2, x3, c)
        x4[block(c)] = finish(2, total[block(c)], x2, c)

    def fill4(i):
        make4(partner(i))

    pl.loop(0, n - 1)(fill4)

    def start4(i):
        out4_copy(i).start()

    inner = jnp.logical_and(me >= half - near, me < half + near)

    @pl.when(inner)
    def _():
        @pl.loop(0, half)
        def _(m):
            start4(across((m + near) % half))

            @pl.when(m < half - 1)
            def _():
                start4(2 * m + 1)

    @pl.when(jnp.logical_not(inner))
    def _():
        near_side(start4)
        far_side(near, half, start4)
        far_side(0, near, start4)

    make4(me)

    def interleave(res, piece, c):
        for l in range(ang // 128):
            res[l, pl.ds(c, rows, stride=n), :] = piece[:, l * 128 : (l + 1) * 128].astype(
                jnp.float32
            )

    interleave(res3, x3[block(me)], me)
    interleave(res4, x4[block(me)], me)

    def arrived3(i):
        out3_copy(i).wait_recv()
        interleave(res3, back3[partner(i)], partner(i))

    def arrived4(i):
        out4_copy(i).wait_recv()
        interleave(res4, back4[partner(i)], partner(i))

    def arrivals(visit):
        near_side(visit)
        far_side(near, half, visit)
        far_side(0, near, visit)

    arrivals(arrived3)

    @pl.loop(0, n - 1)
    def _(i):
        for copy in (pot_copy, new_copy, old_copy, damp_copy, out3_copy):
            copy(i).wait_send()

    @pl.loop(1, hels)
    def _(j):
        pot_share(j).wait_send()

    @pl.when(has_high)
    def _():
        coef_copy.wait_send()

    @pl.loop(0, n)
    def _(c):
        hel_wait_send(0, mine1, c)
        hel_wait_send(1, x2, c)
        hel_wait_send(2, x3, c)

    arrivals(arrived4)

    @pl.loop(0, n - 1)
    def _(i):
        out4_copy(i).wait_send()


def place_kernel(res3, res4, out_old, out_new, sem):
    copies = [
        pltpu.make_async_copy(
            res.at[l], out.at[:, pl.ds(128 * l, 128)], sem.at[s, l]
        )
        for s, (res, out) in enumerate(((res3, out_old), (res4, out_new)))
        for l in range(res.shape[0])
    ]
    for copy in copies:
        copy.start()
    for copy in copies:
        copy.wait()


def one_vibration(
    older_packet, newer_packet, kinetic, transform, potential, coupling, radial_weight, damping
):
    _, rows, n, ang = newer_packet.shape
    hels = lax.axis_size("hel")
    width = ang // hels
    points = n * rows
    bf16, f32 = jnp.bfloat16, jnp.float32
    vector = pltpu.VMEM((points, ang), bf16)
    blocks = pltpu.VMEM((n, rows, ang), bf16)
    wide = pltpu.VMEM((points, ang), f32)
    flat = jax.ShapeDtypeStruct((points, ang), f32)
    anywhere = pl.BlockSpec(memory_space=pl.ANY)
    inside = pl.BlockSpec(memory_space=pltpu.VMEM)
    sem = pltpu.SemaphoreType.DMA
    groups = ang // 128
    result = pltpu.VMEM((groups, points, 128), f32)
    results = pl.pallas_call(
        functools.partial(packet_kernel, n, hels),
        out_shape=(result, result),
        in_specs=[anywhere] * 8,
        out_specs=(inside, inside),
        scratch_shapes=[
            pltpu.VMEM((groups, points, 128), f32),
            pltpu.VMEM((groups, points, 128), f32),
            pltpu.VMEM((points, points), bf16),
            pltpu.VMEM((ang, ang), bf16),
            pltpu.VMEM((rows, n, width), bf16),
            pltpu.VMEM((rows, n, ang), bf16),
            pltpu.VMEM((groups, points, 128), f32),
            pltpu.VMEM((1, ang), bf16),
            pltpu.VMEM((1, ang), bf16),
            pltpu.VMEM((1, rows), f32),
            pltpu.VMEM((n, 1, rows), f32),
            pltpu.VMEM((1, points), f32),
            pltpu.VMEM((points, 128), f32),
            pltpu.VMEM((points, 128), f32),
            pltpu.VMEM((n, rows, width), bf16),
            vector,
            vector,
            vector,
            pltpu.VMEM((hels, points, width), bf16),
            vector,
            vector,
            vector,
            vector,
            vector,
            wide,
            wide,
            vector,
            pltpu.VMEM((STEPS, points, ang), bf16),
            pltpu.VMEM((STEPS, points, ang), bf16),
            blocks,
            blocks,
            sem((7,)),
            sem((2, groups)),
            sem((6, n)),
            sem((6, n)),
            sem((hels,)),
            sem((hels,)),
            sem((STEPS, 2, n)),
            sem((STEPS, 2, n)),
            sem((2,)),
        ],
        compiler_params=pltpu.CompilerParams(
            collective_id=0, has_side_effects=True, vmem_limit_bytes=VMEM_LIMIT
        ),
    )(
        newer_packet.reshape(points, ang),
        older_packet.reshape(points, ang),
        kinetic,
        transform[0],
        potential,
        coupling,
        radial_weight.reshape(1, points),
        damping.reshape(1, rows),
    )
    outs = pl.pallas_call(
        place_kernel,
        out_shape=(flat, flat),
        in_specs=[inside] * 2,
        out_specs=(anywhere, anywhere),
        scratch_shapes=[sem((2, groups))],
        compiler_params=pltpu.CompilerParams(vmem_limit_bytes=4 * 1024 * 1024),
    )(*results)
    shape = newer_packet.shape
    return outs[0].reshape(shape), outs[1].reshape(shape)


def fits(packet):
    hel_rows, rows, vibs, ang = packet.shape
    hels = lax.axis_size("hel")
    return (
        STEPS == 3
        and hel_rows == 1
        and vibs == lax.axis_size("rad")
        and vibs > 1
        and vibs & (vibs - 1) == 0
        and vibs >= 4
        and rows * vibs % 512 == 0
        and hels > 1
        and rows % 16 == 0
        and ang % (hels * 128) == 0
        and rows * vibs <= 512
        and ang <= 1024
    )


def whole_body(older_packet, newer_packet, *rest):
    if fits(newer_packet):
        return one_vibration(older_packet, newer_packet, *rest)
    if newer_packet.shape[2] % lax.axis_size("rad") == 0:
        return by_vibration(older_packet, newer_packet, *rest)
    return body(older_packet, newer_packet, *rest)


def solution(mesh):
    return jax.shard_map(
        whole_body,
        mesh=mesh,
        in_specs=(
            P("hel", "rad", None, None),
            P("hel", "rad", None, None),
            P(),
            P("hel", None, None),
            P("rad", None, None),
            P("hel", None),
            P(),
            P("rad"),
        ),
        out_specs=(P("hel", "rad", None, None), P("hel", "rad", None, None)),
        check_vma=False,
    )
```

```python
import functools

import jax
import jax.numpy as jnp
from jax import lax
from jax.experimental import pallas as pl
from jax.experimental.pallas import tpu as pltpu
from jax.sharding import PartitionSpec as P

STEPS = 3


SCALE_FACTOR = 0.35
VMEM_LIMIT = 60 * 1024 * 1024 - 128 * 1024


def from_behind(array, axis, by):
    devices = lax.axis_size(axis)
    pairs = [(i, i + by) for i in range(devices) if 0 <= i + by < devices]
    return lax.ppermute(array, axis, pairs)


def coriolis_term(block, coefs, weights):
    lower_block, lower_coefs = from_behind((block, coefs), "hel", 1)
    upper_block = from_behind(block, "hel", -1)
    below = jnp.concatenate([lower_block, block[:-1]], axis=0).astype(jnp.float32)
    below_coefs = jnp.concatenate([lower_coefs, coefs[:-1]], axis=0).astype(jnp.float32)
    above = jnp.concatenate([block[1:], upper_block], axis=0).astype(jnp.float32)
    mixed = below_coefs[:, None, :] * below + coefs.astype(jnp.float32)[:, None, :] * above
    return weights[None, :, None] * mixed


def body(
    older_packet, newer_packet, kinetic, transform, potential, coupling, radial_weight, damping
):
    hel_rows, rad_rows, vib_count, ang_count = newer_packet.shape
    flat_width = vib_count * ang_count
    rank = lax.axis_index("rad")
    previous = older_packet.reshape(hel_rows, rad_rows, flat_width)
    current = newer_packet.reshape(hel_rows, rad_rows, flat_width)
    potential_flat = potential.astype(jnp.float32).reshape(1, rad_rows * vib_count, ang_count)
    tiled_coefs = jnp.tile(coupling, (1, vib_count))
    damp = damping[None, :, None]
    for _ in range(STEPS):
        rounded = current.astype(jnp.bfloat16)
        regrouped = lax.all_to_all(rounded, "rad", split_axis=2, concat_axis=1, tiled=True)
        kinetic_term = jnp.einsum(
            "rs,ksc->krc", kinetic, regrouped, preferred_element_type=jnp.float32
        )
        returned = lax.all_to_all(kinetic_term, "rad", split_axis=1, concat_axis=2, tiled=True)
        start = rank * rad_rows
        local_weights = lax.dynamic_slice_in_dim(radial_weight, start, rad_rows, 0)
        summed = returned + coriolis_term(rounded, tiled_coefs, local_weights)
        off_grid = summed.astype(jnp.bfloat16).astype(jnp.float32)
        angular_rows = rounded.reshape(hel_rows, rad_rows * vib_count, ang_count)
        grid = jnp.einsum(
            "kna,kag->kng", angular_rows, transform, preferred_element_type=jnp.float32
        )
        grid_values = (grid * potential_flat).astype(jnp.bfloat16)
        angular_part = jnp.einsum(
            "kng,kag->kna", grid_values, transform, preferred_element_type=jnp.float32
        )
        applied = SCALE_FACTOR * (off_grid + angular_part.reshape(hel_rows, rad_rows, flat_width))
        following = damp * (2.0 * applied - damp * previous)
        previous = current
        current = following
    shape = (hel_rows, rad_rows, vib_count, ang_count)
    return (previous.reshape(shape), current.reshape(shape))


def by_vibration(
    older_packet, newer_packet, kinetic, transform, potential, coupling, radial_weight, damping
):
    hel_rows, rad_rows, vib_count, ang_count = newer_packet.shape
    devices = lax.axis_size("rad")

    def scatter(array):
        return lax.all_to_all(array, "rad", split_axis=2, concat_axis=1, tiled=True)

    rounded = scatter(newer_packet.astype(jnp.bfloat16))
    previous = scatter(older_packet.astype(jnp.bfloat16)).astype(jnp.float32)
    pot = scatter(potential[None])[0].astype(jnp.float32)
    damp = lax.all_gather(damping, "rad", tiled=True)[None, :, None, None]
    weight = radial_weight[None, :, None, None]
    current = rounded.astype(jnp.float32)
    lower_coefs = from_behind(coupling, "hel", 1)
    coefs = jnp.concatenate([lower_coefs, coupling], axis=0).astype(jnp.float32)
    coefs = coefs[:, None, None, :]
    history = []
    for step in range(STEPS):
        lower = from_behind(rounded[-1:], "hel", 1)
        upper = from_behind(rounded[:1], "hel", -1)
        padded = jnp.concatenate([lower, rounded, upper], axis=0).astype(jnp.float32)
        mixed = coefs[:-1] * padded[:-2] + coefs[1:] * padded[2:]
        radial = jnp.einsum(
            "rs,ksva->krva", kinetic, rounded, preferred_element_type=jnp.float32
        )
        off_grid = radial + weight * mixed
        grid = jnp.einsum(
            "krva,kag->krvg", rounded, transform, preferred_element_type=jnp.float32
        )
        grid_values = (grid * pot[None]).astype(jnp.bfloat16)
        angular = jnp.einsum(
            "krvg,kag->krva", grid_values, transform, preferred_element_type=jnp.float32
        )
        applied = SCALE_FACTOR * (off_grid + angular)
        following = damp * (2.0 * applied - damp * previous)
        previous = current
        current = following
        rounded = current.astype(jnp.bfloat16)
        history.append(rounded)

    def gather(array):
        back = lax.all_to_all(array, "rad", split_axis=1, concat_axis=2, tiled=True)
        return back.astype(jnp.float32)

    return gather(history[-2]), gather(history[-1])


MESH = pl.DeviceIdType.MESH
POT, NEW, OLD, DAMP, OUT3, OUT4 = range(6)


def xor(a, b, n):
    bit, total = 1, 0
    while bit < n:
        total = total + bit * ((a // bit + b // bit) % 2)
        bit *= 2
    return total


def packet_kernel(
    n, hels,
    newer, older, kinetic, transform, potential, coupling, weight, damping,
    res3, res4,
    newer_v, older_v, kin, tr, pot_in, pot_full, pot_wide, coef, coef_low, damp_own, damp_all,
    weight_all, damp_col, weight_col, send_pot, pot_mine, mine0, mine1, pot, x0, x1, x2, x3, x4,
    total, second, grid, low, high, back3, back4,
    in_sem, lane_sem, rad_send, rad_recv, pot_send, pot_recv, hel_send, hel_recv, coef_sem,
):
    me = lax.axis_index("rad")
    hel = lax.axis_index("hel")
    rows = send_pot.shape[1]
    ang = newer.shape[1]
    width = ang // hels
    half = n // 2
    far = half // 2
    near = half - far
    side = me // half
    has_low = hel > 0
    has_high = hel < hels - 1

    def partner(i):
        odd = i % 2
        return xor(me, odd * ((i + 1) // 2) + (1 - odd) * (half + i // 2), n)

    def across(s):
        s = xor(s, me % near, half)
        return 2 * xor(me % half, s + side * (half - 1 - 2 * s), half)

    def block(c):
        return pl.ds(pl.multiple_of(c * rows, rows), rows)

    barrier = pltpu.get_barrier_semaphore()

    @pl.loop(1, n)
    def _(j):
        pl.semaphore_signal(
            barrier, inc=1, device_id={"rad": lax.rem(me + j, n)}, device_id_type=MESH
        )

    @pl.loop(1, hels)
    def _(j):
        pl.semaphore_signal(
            barrier, inc=1, device_id={"hel": lax.rem(hel + j, hels)}, device_id_type=MESH
        )

    loads = [
        pltpu.make_async_copy(src, dst, in_sem.at[s])
        for s, (src, dst) in enumerate(
            (
                (potential.at[:, :, pl.ds(pl.multiple_of(hel * width, width), width)], pot_in),
                (damping, damp_own),
                (coupling, coef),
                (weight, weight_all),
                (transform, tr),
                (potential, pot_full),
                (kinetic, kin),
            )
        )
    ]

    def lanes(l):
        return pl.ds(pl.multiple_of(l * 128, 128), 128)

    def newer_load(l):
        return pltpu.make_async_copy(newer.at[:, lanes(l)], newer_v.at[l], lane_sem.at[0, l])

    def older_load(l):
        return pltpu.make_async_copy(older.at[:, lanes(l)], older_v.at[l], lane_sem.at[1, l])

    def each_lane(copy, method):
        @pl.loop(0, ang // 128)
        def _(l):
            getattr(copy(l), method)()

    for load in loads[:3]:
        load.start()
    each_lane(newer_load, "start")
    each_lane(older_load, "start")
    for load in loads[3:]:
        load.start()

    pl.semaphore_wait(barrier, n + hels - 2)

    def over_rad(kind, src, dst, i):
        return pltpu.make_async_remote_copy(
            src_ref=src,
            dst_ref=dst,
            send_sem=rad_send.at[kind, i],
            recv_sem=rad_recv.at[kind, i],
            device_id={"rad": partner(i)},
            device_id_type=MESH,
        )

    def pot_copy(i):
        return over_rad(POT, send_pot.at[i], pot.at[hel, block(me)], i)

    def new_copy(i):
        return over_rad(NEW, mine1.at[block(partner(i))], x1.at[block(me)], i)

    def old_copy(i):
        return over_rad(OLD, mine0.at[block(partner(i))], x0.at[block(me)], i)

    def damp_copy(i):
        return over_rad(DAMP, damp_own, damp_all.at[me], i)

    def out3_copy(i):
        return over_rad(OUT3, x3.at[block(partner(i))], back3.at[me], i)

    def out4_copy(i):
        return over_rad(OUT4, x4.at[block(partner(i))], back4.at[me], i)

    def pot_share(j):
        return pltpu.make_async_remote_copy(
            src_ref=pot.at[hel],
            dst_ref=pot.at[hel],
            send_sem=pot_send.at[j],
            recv_sem=pot_recv.at[j],
            device_id={"hel": lax.rem(hel + j, hels)},
            device_id_type=MESH,
        )

    coef_copy = pltpu.make_async_remote_copy(
        src_ref=coef,
        dst_ref=coef_low,
        send_sem=coef_sem.at[0],
        recv_sem=coef_sem.at[1],
        device_id={"hel": lax.rem(hel + 1, hels)},
        device_id_type=MESH,
    )

    def hel_up(step, x, c):
        return pltpu.make_async_remote_copy(
            src_ref=x.at[block(c)],
            dst_ref=low.at[step, block(c)],
            send_sem=hel_send.at[step, 0, c],
            recv_sem=hel_recv.at[step, 0, c],
            device_id={"hel": lax.rem(hel + 1, hels)},
            device_id_type=MESH,
        )

    def hel_down(step, x, c):
        return pltpu.make_async_remote_copy(
            src_ref=x.at[block(c)],
            dst_ref=high.at[step, block(c)],
            send_sem=hel_send.at[step, 1, c],
            recv_sem=hel_recv.at[step, 1, c],
            device_id={"hel": lax.rem(hel - 1 + hels, hels)},
            device_id_type=MESH,
        )

    def hel_start(step, x, c):
        @pl.when(has_high)
        def _():
            hel_up(step, x, c).start()

        @pl.when(has_low)
        def _():
            hel_down(step, x, c).start()

    def hel_wait_recv(step, x, c):
        @pl.when(has_low)
        def _():
            hel_up(step, x, c).wait_recv()

        @pl.when(has_high)
        def _():
            hel_down(step, x, c).wait_recv()

    def hel_wait_send(step, x, c):
        @pl.when(has_high)
        def _():
            hel_up(step, x, c).wait_send()

        @pl.when(has_low)
        def _():
            hel_down(step, x, c).wait_send()

    def near_first(visit):
        @pl.loop(0, half)
        def _(s):
            visit(across(s))

            @pl.when(s < half - 1)
            def _():
                visit(2 * s + 1)

    loads[0].wait()
    for l in range(width // 128):
        part = pot_in[:, :, 128 * l : 128 * (l + 1)].astype(jnp.float32)
        pot_wide[l] = part.reshape(pot_wide.shape[1:])

    def picked(ref, c, count):
        return jnp.concatenate(
            [ref[l, pl.ds(c, rows, stride=n), :] for l in range(count)], axis=1
        )

    def make_pot(i):
        send_pot[i] = picked(pot_wide, partner(i), width // 128).astype(jnp.bfloat16)

    def send_pots(i):
        make_pot(i)
        pot_copy(i).start()

    near_first(send_pots)
    pot[hel, block(me)] = picked(pot_wide, me, width // 128).astype(jnp.bfloat16)

    each_lane(newer_load, "wait")

    def make_new(i):
        mine1[block(partner(i))] = picked(newer_v, partner(i), ang // 128).astype(jnp.bfloat16)

    def send_new(i):
        make_new(i)
        new_copy(i).start()

    near_first(send_new)
    mine1[block(me)] = picked(newer_v, me, ang // 128).astype(jnp.bfloat16)

    @pl.loop(0, n)
    def _(c):
        hel_start(0, mine1, c)

    x1[block(me)] = mine1[block(me)]
    loads[1].wait()
    loads[2].wait()

    @pl.loop(0, n - 1)
    def _(i):
        damp_copy(i).start()

    @pl.when(has_high)
    def _():
        coef_copy.start()

    damp_all[me] = damp_own[...]

    @pl.when(jnp.logical_not(has_low))
    def _():
        low[...] = jnp.zeros_like(low)
        coef_low[...] = jnp.zeros_like(coef_low)

    @pl.when(jnp.logical_not(has_high))
    def _():
        high[...] = jnp.zeros_like(high)

    line = lax.broadcasted_iota(jnp.int32, (rows, rows), 0)
    lane = lax.broadcasted_iota(jnp.int32, (rows, rows), 1)

    def column(row):
        diagonal = jnp.where(line == lane, jnp.broadcast_to(row, (rows, rows)), 0.0)
        return jnp.broadcast_to(jnp.sum(diagonal, axis=1, keepdims=True), (rows, 128))

    damp_col[block(me)] = column(damp_own[...])
    loads[3].wait()
    for c in range(n):
        part = weight_all[:, c * rows : (c + 1) * rows]
        weight_col[c * rows : (c + 1) * rows] = column(part)

    loads[4].wait()
    loads[5].wait()
    for l in range(ang // 128):
        part = pot_full[:, :, 128 * l : 128 * (l + 1)].astype(jnp.float32)
        pot_wide[l] = part.reshape(pot_wide.shape[1:])

    @pl.loop(0, n)
    def _(c):
        pot_mine[block(c)] = picked(pot_wide, c, ang // 128).astype(jnp.bfloat16)

    everything = pl.ds(0, n * rows)

    def from_grid(span):
        return lax.dot_general(
            grid[span], tr[...], (((1,), (1,)), ((), ())), preferred_element_type=jnp.float32
        )

    values = jnp.dot(mine1[...], tr[...], preferred_element_type=jnp.float32)
    grid[...] = (values * pot_mine[...].astype(jnp.float32)).astype(jnp.bfloat16)
    total[...] = from_grid(everything)

    @pl.loop(0, n - 1)
    def _(i):
        pot_copy(i).wait_recv()

    @pl.loop(1, hels)
    def _(j):
        pot_share(j).start()

    @pl.when(has_low)
    def _():
        coef_copy.wait_recv()

    lower_coef = coef_low[...].astype(jnp.float32)
    upper_coef = coef[...].astype(jnp.float32)

    def mixed(step, span):
        below = lower_coef * low[step, span].astype(jnp.float32)
        return below + upper_coef * high[step, span].astype(jnp.float32)

    each_lane(older_load, "wait")
    my_damp = damp_col[block(me), 0:1]
    my_weight = weight_col[block(me), 0:1]

    def make_old(c):
        hel_wait_recv(0, mine1, c)
        applied = SCALE_FACTOR * (total[block(c)] + my_weight * mixed(0, block(c)))
        prev = picked(older_v, c, ang // 128)
        mine0[block(c)] = (my_damp * (2.0 * applied - my_damp * prev)).astype(jnp.bfloat16)

    def send_old(i):
        make_old(partner(i))
        old_copy(i).start()

    near_first(send_old)

    make_old(me)
    x0[block(me)] = mine0[block(me)]

    @pl.loop(0, n - 1)
    def _(i):
        damp_copy(i).wait_recv()

    @pl.loop(0, n)
    def _(c):
        damp_col[block(c)] = column(damp_all[c])

    def near_side(visit):
        @pl.loop(0, half - 1)
        def _(m):
            visit(2 * m + 1)

    def far_side(first, last, visit):
        @pl.loop(first, last)
        def _(s):
            visit(across(s))

    loads[6].wait()

    @pl.loop(0, n - 1)
    def _(i):
        new_copy(i).wait_recv()

    total[...] = jnp.dot(kin[...], x1[...], preferred_element_type=jnp.float32)

    @pl.loop(1, hels)
    def _(j):
        pot_share(j).wait_recv()

    def to_grid(x, span):
        values = jnp.dot(x[span], tr[...], preferred_element_type=jnp.float32)
        for t in range(hels):
            part = values[:, t * width : (t + 1) * width] * pot[t, span].astype(jnp.float32)
            grid[span, t * width : (t + 1) * width] = part.astype(jnp.bfloat16)

    def multiply(x):
        to_grid(x, everything)
        radial = jnp.dot(kin[...], x[...], preferred_element_type=jnp.float32)
        total[...] = from_grid(everything) + radial

    def finish(step, whole, prev, c):
        span = block(c)
        damp = damp_col[span, 0:1]
        applied = SCALE_FACTOR * (whole + weight_col[span, 0:1] * mixed(step, span))
        following = damp * (2.0 * applied - damp * prev[span].astype(jnp.float32))
        return following.astype(jnp.bfloat16)

    def advance(c):
        span = block(c)
        scale = 2.0 * SCALE_FACTOR * damp_col[span, 0:1]
        x2[span] = (scale * total[span] + x0[span].astype(jnp.float32)).astype(jnp.bfloat16)
        hel_start(1, x2, c)

    def stretch(first, count):
        return pl.ds(pl.multiple_of(first * rows, count * rows), count * rows)

    ours = stretch(side * half, half)
    early = stretch((1 - side) * (half + near), far)
    late = stretch(half - side * near, near)

    def spread(to, source):
        return jnp.dot(kin[to, source], x2[source], preferred_element_type=jnp.float32)

    def turn(span):
        to_grid(x2, span)
        second[span] += from_grid(span)

    def old_arrived(i):
        old_copy(i).wait_recv()
        advance(partner(i))

    advance(me)
    near_side(old_arrived)
    second[...] = spread(everything, ours)
    turn(ours)
    far_side(near, half, old_arrived)
    second[...] += spread(everything, early)
    turn(early)
    far_side(0, near, old_arrived)

    def make3(c):
        hel_wait_recv(1, x2, c)
        x3[block(c)] = finish(1, second[block(c)], x1, c)

    def send3(i):
        make3(partner(i))
        out3_copy(i).start()

    second[early] += spread(early, late)
    far_side(near, half, send3)
    second[ours] += spread(ours, late)
    send3(1)
    second[late] += spread(late, late)
    turn(late)

    @pl.loop(0, near)
    def _(s):
        send3(across(s))

        @pl.when(s + 2 < half)
        def _():
            send3(2 * s + 3)

    @pl.loop(near + 1, half - 1)
    def _(m):
        send3(2 * m + 1)

    make3(me)

    @pl.loop(0, n)
    def _(c):
        hel_start(2, x3, c)

    multiply(x3)

    def make4(c):
        hel_wait_recv(2, x3, c)
        x4[block(c)] = finish(2, total[block(c)], x2, c)

    def fill4(i):
        make4(partner(i))

    pl.loop(0, n - 1)(fill4)

    def start4(i):
        out4_copy(i).start()

    inner = jnp.logical_and(me >= half - near, me < half + near)

    @pl.when(inner)
    def _():
        @pl.loop(0, half)
        def _(m):
            start4(across((m + near) % half))

            @pl.when(m < half - 1)
            def _():
                start4(2 * m + 1)

    @pl.when(jnp.logical_not(inner))
    def _():
        near_side(start4)
        far_side(near, half, start4)
        far_side(0, near, start4)

    make4(me)

    def interleave(res, piece, c):
        for l in range(ang // 128):
            res[l, pl.ds(c, rows, stride=n), :] = piece[:, l * 128 : (l + 1) * 128].astype(
                jnp.float32
            )

    interleave(res3, x3[block(me)], me)
    interleave(res4, x4[block(me)], me)

    def arrived3(i):
        out3_copy(i).wait_recv()
        interleave(res3, back3[partner(i)], partner(i))

    def arrived4(i):
        out4_copy(i).wait_recv()
        interleave(res4, back4[partner(i)], partner(i))

    def arrivals(visit):
        near_side(visit)
        far_side(near, half, visit)
        far_side(0, near, visit)

    arrivals(arrived3)

    @pl.loop(0, n - 1)
    def _(i):
        for copy in (pot_copy, new_copy, old_copy, damp_copy, out3_copy):
            copy(i).wait_send()

    @pl.loop(1, hels)
    def _(j):
        pot_share(j).wait_send()

    @pl.when(has_high)
    def _():
        coef_copy.wait_send()

    @pl.loop(0, n)
    def _(c):
        hel_wait_send(0, mine1, c)
        hel_wait_send(1, x2, c)
        hel_wait_send(2, x3, c)

    arrivals(arrived4)

    @pl.loop(0, n - 1)
    def _(i):
        out4_copy(i).wait_send()


def place_kernel(res3, res4, out_old, out_new, sem):
    copies = [
        pltpu.make_async_copy(
            res.at[l], out.at[:, pl.ds(128 * l, 128)], sem.at[s, l]
        )
        for s, (res, out) in enumerate(((res3, out_old), (res4, out_new)))
        for l in range(res.shape[0])
    ]
    for copy in copies:
        copy.start()
    for copy in copies:
        copy.wait()


def one_vibration(
    older_packet, newer_packet, kinetic, transform, potential, coupling, radial_weight, damping
):
    _, rows, n, ang = newer_packet.shape
    hels = lax.axis_size("hel")
    width = ang // hels
    points = n * rows
    bf16, f32 = jnp.bfloat16, jnp.float32
    vector = pltpu.VMEM((points, ang), bf16)
    blocks = pltpu.VMEM((n, rows, ang), bf16)
    wide = pltpu.VMEM((points, ang), f32)
    flat = jax.ShapeDtypeStruct((points, ang), f32)
    anywhere = pl.BlockSpec(memory_space=pl.ANY)
    inside = pl.BlockSpec(memory_space=pltpu.VMEM)
    sem = pltpu.SemaphoreType.DMA
    groups = ang // 128
    result = pltpu.VMEM((groups, points, 128), f32)
    results = pl.pallas_call(
        functools.partial(packet_kernel, n, hels),
        out_shape=(result, result),
        in_specs=[anywhere] * 8,
        out_specs=(inside, inside),
        scratch_shapes=[
            pltpu.VMEM((groups, points, 128), f32),
            pltpu.VMEM((groups, points, 128), f32),
            pltpu.VMEM((points, points), bf16),
            pltpu.VMEM((ang, ang), bf16),
            pltpu.VMEM((rows, n, width), bf16),
            pltpu.VMEM((rows, n, ang), bf16),
            pltpu.VMEM((groups, points, 128), f32),
            pltpu.VMEM((1, ang), bf16),
            pltpu.VMEM((1, ang), bf16),
            pltpu.VMEM((1, rows), f32),
            pltpu.VMEM((n, 1, rows), f32),
            pltpu.VMEM((1, points), f32),
            pltpu.VMEM((points, 128), f32),
            pltpu.VMEM((points, 128), f32),
            pltpu.VMEM((n, rows, width), bf16),
            vector,
            vector,
            vector,
            pltpu.VMEM((hels, points, width), bf16),
            vector,
            vector,
            vector,
            vector,
            vector,
            wide,
            wide,
            vector,
            pltpu.VMEM((STEPS, points, ang), bf16),
            pltpu.VMEM((STEPS, points, ang), bf16),
            blocks,
            blocks,
            sem((7,)),
            sem((2, groups)),
            sem((6, n)),
            sem((6, n)),
            sem((hels,)),
            sem((hels,)),
            sem((STEPS, 2, n)),
            sem((STEPS, 2, n)),
            sem((2,)),
        ],
        compiler_params=pltpu.CompilerParams(
            collective_id=0, has_side_effects=True, vmem_limit_bytes=VMEM_LIMIT
        ),
    )(
        newer_packet.reshape(points, ang),
        older_packet.reshape(points, ang),
        kinetic,
        transform[0],
        potential,
        coupling,
        radial_weight.reshape(1, points),
        damping.reshape(1, rows),
    )
    outs = pl.pallas_call(
        place_kernel,
        out_shape=(flat, flat),
        in_specs=[inside] * 2,
        out_specs=(anywhere, anywhere),
        scratch_shapes=[sem((2, groups))],
        compiler_params=pltpu.CompilerParams(vmem_limit_bytes=4 * 1024 * 1024),
    )(*results)
    shape = newer_packet.shape
    return outs[0].reshape(shape), outs[1].reshape(shape)


def fits(packet):
    hel_rows, rows, vibs, ang = packet.shape
    hels = lax.axis_size("hel")
    return (
        STEPS == 3
        and hel_rows == 1
        and vibs == lax.axis_size("rad")
        and vibs > 1
        and vibs & (vibs - 1) == 0
        and vibs >= 4
        and rows * vibs % 512 == 0
        and hels > 1
        and rows % 16 == 0
        and ang % (hels * 128) == 0
        and rows * vibs <= 512
        and ang <= 1024
    )


def whole_body(older_packet, newer_packet, *rest):
    if fits(newer_packet):
        return one_vibration(older_packet, newer_packet, *rest)
    if newer_packet.shape[2] % lax.axis_size("rad") == 0:
        return by_vibration(older_packet, newer_packet, *rest)
    return body(older_packet, newer_packet, *rest)


def solution(mesh):
    return jax.shard_map(
        whole_body,
        mesh=mesh,
        in_specs=(
            P("hel", "rad", None, None),
            P("hel", "rad", None, None),
            P(),
            P("hel", None, None),
            P("rad", None, None),
            P("hel", None),
            P(),
            P("rad"),
        ),
        out_specs=(P("hel", "rad", None, None), P("hel", "rad", None, None)),
        check_vma=False,
    )
```
